32 devices in a mesh: tok: 4 (over y, core), feat: 8 (over z, x).
Axes of the slice: x: 2, y: 2, z: 4, core: 2. Of those that a mesh axis runs over, the one named last changes fastest.
Arguments:
- tokens: bfloat16 [4096, 2048], P('tok', 'feat'), may hold values from -6 to 6
- level_bits: int32 [2, 4], replicated, may hold values from 0 to 3, each once within a row
- up_blocks: bfloat16 [2, 16, 5, 128, 512], P(None, 'feat', None, None, 'tok'), may hold values from -0.21875 to 0.21875
- down_blocks: bfloat16 [2, 16, 5, 512, 128], P(None, 'feat', None, None, 'tok'), may hold values from -0.109375 to 0.109375
- rank_in: bfloat16 [2, 2048, 256], replicated, may hold values from -0.125 to 0.125
- rank_up: bfloat16 [2, 256, 8192], P(None, None, 'feat'), may hold values from -0.15625 to 0.15625
- rank_down: bfloat16 [2, 8192, 256], P(None, 'feat'), may hold values from -0.0625 to 0.0625
- rank_out: bfloat16 [2, 256, 2048], P(None, None, 'feat'), may hold values from -0.15625 to 0.15625
Outputs:
- outputs: bfloat16 [4096, 2048], P('tok', 'feat')
The draws below stay inside these ranges and needn't reach their ends.
Inputs may be any that keep to these rules, and one draw needn't show every extreme that they name: `level_bits`: each row is a permutation of the bits 0 to 3.
All inputs are finite; a program needn't handle non-finite values.
Results may differ from the reference program's by a relative error of at most 0.015.
Values may be sent and summed in bfloat16 or wider, within the bound.
A program may use at most 64 MiB of HBM per device.

```python
import jax
import jax.numpy as jnp
from jax import lax

D = 2048
HID = 8192
NB = 16
LEVELS = 4
RANK = 256
LAYERS = 2
TOK_DEV = 1024
TOKENS = 4096


def levels(rng, shape, cuts, smallest, largest):
    level = 1.0
    for dim, shards_of in cuts:
        heights = jax.random.uniform(jax.random.fold_in(jax.random.fold_in(rng, 6), dim), (shards_of,), jnp.float32, smallest / len(cuts), largest / len(cuts))
        level = level * jnp.repeat(jnp.exp(heights), shape[dim] // shards_of).reshape((-1,) + (1,) * (len(shape) - 1 - dim))
    return level


def centred(key, dims, scale, most, pieces=(), kind=jnp.bfloat16):
    drawn = jax.random.normal(key, dims, jnp.float32) * scale
    if len(pieces) > 0:
        drawn = levels(key, dims, pieces, -0.22, 0.18) * drawn
    return jnp.clip(drawn, min=-most, max=most).astype(kind)


def setup_inputs(seed: int = 0) -> dict:
    seeds = jax.random.split(jax.random.key(seed), 9)
    tokens = centred(seeds[0], (TOKENS, D), 1.0, 6.0, ((0, 4), (1, 8)))
    level_bits = jax.vmap(lambda own: jax.random.permutation(own, LEVELS))(jax.random.split(seeds[1], LAYERS)).reshape((LAYERS, LEVELS)).astype(jnp.int32)
    up_blocks = centred(seeds[2], (LAYERS, NB, LEVELS + 1, D // NB, HID // NB), ((LEVELS + 2) * (D // NB)) ** -0.5, 0.21875, ((1, 8), (4, 4)))
    down_blocks = centred(seeds[3], (LAYERS, NB, LEVELS + 1, HID // NB, D // NB), ((LEVELS + 2) * (HID // NB)) ** -0.5, 0.109375, ((1, 8), (4, 4)))
    rank_in = centred(seeds[4], (LAYERS, D, RANK), D ** -0.5, 0.125)
    rank_up = centred(seeds[5], (LAYERS, RANK, HID), ((LEVELS + 2) * RANK) ** -0.5, 0.15625, ((2, 8),))
    rank_down = centred(seeds[6], (LAYERS, HID, RANK), HID ** -0.5, 0.0625, ((1, 8),))
    rank_out = centred(seeds[7], (LAYERS, RANK, D), ((LEVELS + 2) * RANK) ** -0.5, 0.15625, ((2, 8),))
    return {"tokens": tokens, "level_bits": level_bits, "up_blocks": up_blocks, "down_blocks": down_blocks, "rank_in": rank_in, "rank_up": rank_up, "rank_down": rank_down, "rank_out": rank_out}


def block_einsum(left, right):
    return jnp.einsum("tjd,jdh->tjh", left.astype(jnp.float32), right.astype(jnp.float32))


def reference(tokens, level_bits, up_blocks, down_blocks, rank_in, rank_up, rank_down, rank_out):
    width_block = D // NB
    hidden_block = HID // NB
    block_ids = jnp.arange(NB, dtype=jnp.int32)
    current = tokens
    for layer_num in range(LAYERS):
        up_layer = up_blocks[layer_num]
        down_layer = down_blocks[layer_num]
        partners = [jnp.bitwise_xor(block_ids, jnp.left_shift(jnp.int32(1), level_bits[layer_num, level_num]).astype(jnp.int32)).astype(jnp.int32) for level_num in range(LEVELS)]

        def tile_layer(tile_rows, up_layer=up_layer, down_layer=down_layer, partners=partners, layer_num=layer_num):
            blocked = tile_rows.reshape(-1, NB, width_block)
            pre_act = block_einsum(blocked, up_layer[:, 0])
            for level_num in range(LEVELS):
                partner = jnp.take(blocked, partners[level_num], axis=1)
                pre_act = pre_act + block_einsum(partner, up_layer[:, 1 + level_num])
            latent = jnp.dot(tile_rows, rank_in[layer_num], preferred_element_type=jnp.float32).astype(jnp.bfloat16)
            pre_act = pre_act + jnp.dot(latent, rank_up[layer_num], preferred_element_type=jnp.float32).reshape(-1, NB, hidden_block)
            hidden = jax.nn.gelu(pre_act, approximate=False).astype(jnp.bfloat16)
            result = block_einsum(hidden, down_layer[:, 0])
            for level_num in range(LEVELS):
                moved = jnp.take(hidden, partners[level_num], axis=1)
                moved_weight = jnp.take(down_layer[:, 1 + level_num], partners[level_num], axis=0)
                result = result + block_einsum(moved, moved_weight)
            latent_back = jnp.dot(hidden.reshape(-1, HID), rank_down[layer_num], preferred_element_type=jnp.float32).astype(jnp.bfloat16)
            result = result + jnp.dot(latent_back, rank_out[layer_num], preferred_element_type=jnp.float32).reshape(-1, NB, width_block)
            return (tile_rows.astype(jnp.float32) + result.reshape(-1, D)).astype(jnp.bfloat16)

        tiles = current.reshape(TOKENS // TOK_DEV, TOK_DEV, D)
        current = lax.map(tile_layer, tiles).reshape(TOKENS, D)
    return current
```

```python
import functools
import math

import jax
import jax.numpy as jnp
from jax import lax
from jax.experimental import pallas as pl
from jax.experimental.pallas import tpu as pltpu
from jax.sharding import PartitionSpec as P

CHUNK_ROWS = 256
LINE_CHUNK = 128
SKEW = 1
LATER = 1
MESH = pl.DeviceIdType.MESH


def bits_of(count):
    return count.bit_length() - 1


def network(cfg, tokens, level_bits, up_in, down_in, rank_in, rank_up, rank_down, rank_out, out, *scratch):
    (xbuf, xrecv, tsend, trecv, part, half, full, hid, acc, wup, wdown) = scratch[:11]
    rest = scratch[11:]
    layers, rows, width = cfg["layers"], cfg["rows"], cfg["width"]
    blocks, wb, hb = cfg["blocks"], cfg["wb"], cfg["hb"]
    n_feat, n_tok, rank = cfg["n_feat"], cfg["n_tok"], cfg["rank"]
    cr = cfg["chunk"]
    chunks = rows // cr
    local_bits = bits_of(blocks)
    nb = bits_of(n_feat)
    levels = local_bits + nb
    gather = cfg["gather"]
    if gather:
        upg, downg = rest[:layers], rest[layers : 2 * layers]
        wsend, wrecv, wloc = rest[2 * layers : 2 * layers + 3]
        rest = rest[2 * layers + 3 :]
    else:
        upg = [up_in.at[l] for l in range(layers)]
        downg = [down_in.at[l] for l in range(layers)]
    xs_sem, xr_sem, ts_sem, tr_sem, as_sem, ar_sem = rest

    me = lax.axis_index("feat")
    me_tok = lax.axis_index("tok")
    mybit = [(me // (1 << b)) % 2 for b in range(nb)]
    partner = [me + (1 << b) * (1 - 2 * mybit[b]) for b in range(nb)]

    barrier = pltpu.get_barrier_semaphore()
    for b in range(nb):
        pl.semaphore_signal(barrier, inc=1, device_id={"feat": partner[b]}, device_id_type=MESH)
    greeted = nb
    if gather:
        for o in range(1, n_tok):
            pl.semaphore_signal(
                barrier, inc=1, device_id={"tok": lax.rem(me_tok + o, n_tok)}, device_id_type=MESH
            )
        greeted += n_tok - 1
    pl.semaphore_wait(barrier, greeted)

    def weight_copy(l, kind, o):
        if kind == 0:
            cols = up_in.shape[-1]
            src = up_in.at[l]
            dst = upg[l].at[:, :, :, pl.ds(pl.multiple_of(me_tok * cols, cols), cols)]
        else:
            cols = down_in.shape[-2]
            src = down_in.at[l]
            dst = downg[l].at[:, :, pl.ds(pl.multiple_of(me_tok * cols, cols), cols), :]
        if o == 0:
            return pltpu.make_async_copy(src, dst, wloc.at[l, kind])
        return pltpu.make_async_remote_copy(
            src_ref=src,
            dst_ref=dst,
            send_sem=wsend.at[l, kind, o - 1],
            recv_sem=wrecv.at[l, kind, o - 1],
            device_id={"tok": lax.rem(me_tok + o, n_tok)},
            device_id_type=MESH,
        )

    def start_weights():
        for l in range(layers):
            for kind in range(2):
                for o in range(n_tok):
                    weight_copy(l, kind, o).start()

    prepared = set()

    def prepare(l, kind):
        if (l, kind) in prepared:
            return
        prepared.add((l, kind))
        if gather:
            for o in range(n_tok):
                copy = weight_copy(l, kind, o)
                copy.wait() if o == 0 else copy.wait_recv()
        order = []
        for b in range(levels):
            at = 0
            for k in range(levels):
                at = jnp.maximum(at, jnp.where(level_bits[l, k] == b, 1 + k, 0))
            order.append(at)
        for j in range(blocks):
            if kind == 0:
                wup[l, j, pl.ds(0, wb), :] = upg[l][j, 0]
                for b in range(levels):
                    wup[l, j, pl.ds((1 + b) * wb, wb), :] = upg[l][j, order[b]]
                wup[l, j, pl.ds((1 + levels) * wb, rank), :] = rank_up[l, :, pl.ds(j * hb, hb)]
            else:
                wdown[l, j, pl.ds(0, wb), :] = downg[l][j, 0]
                for b in range(levels):
                    wdown[l, j, pl.ds((1 + b) * wb, wb), :] = downg[l][j, order[b]]

    def x_copy(l, c, b):
        at = pl.ds(c * cr, cr)
        return pltpu.make_async_remote_copy(
            src_ref=xbuf.at[l, at, :],
            dst_ref=xrecv.at[l, b, at, :],
            send_sem=xs_sem.at[l, c, b],
            recv_sem=xr_sem.at[l, c, b],
            device_id={"feat": partner[b]},
            device_id_type=MESH,
        )

    def t_copy(l, c, b):
        at = pl.ds(c * cr, cr)
        return pltpu.make_async_remote_copy(
            src_ref=tsend.at[l, b, at, :],
            dst_ref=trecv.at[l, b, at, :],
            send_sem=ts_sem.at[l, c, b],
            recv_sem=tr_sem.at[l, c, b],
            device_id={"feat": partner[b]},
            device_id_type=MESH,
        )

    last = nb - 1
    sizes = [cr >> (k + 1) for k in range(last)]
    own_at = [0]
    for k in range(last):
        own_at.append(own_at[-1] + mybit[k] * sizes[k])
    away_at = [own_at[k] + (1 - mybit[k]) * sizes[k] for k in range(last)]
    piece = cr >> last
    half_at = [sum(sizes[:k]) for k in range(last + 1)]
    half_rows = half_at[-1] + piece

    def reduce_copy(u, c, k):
        if k < last:
            src = part.at[u, pl.ds(pl.multiple_of(c * cr + away_at[k], sizes[k]), sizes[k]), :]
            size = sizes[k]
        else:
            src = part.at[u, pl.ds(pl.multiple_of(c * cr + own_at[last], piece), piece), :]
            size = piece
        return pltpu.make_async_remote_copy(
            src_ref=src,
            dst_ref=half.at[u, pl.ds(c * half_rows + half_at[k], size), :],
            send_sem=as_sem.at[u, c, k],
            recv_sem=ar_sem.at[u, c, k],
            device_id={"feat": partner[k]},
            device_id_type=MESH,
        )

    def spread_copy(u, c, k):
        size = cr >> (k + 1)
        at = pl.ds(pl.multiple_of(c * cr + own_at[k + 1], size), size)
        return pltpu.make_async_remote_copy(
            src_ref=full.at[u, at, :],
            dst_ref=full.at[u, at, :],
            send_sem=as_sem.at[u, c, nb + k],
            recv_sem=ar_sem.at[u, c, nb + k],
            device_id={"feat": partner[k]},
            device_id_type=MESH,
        )

    def start_bulk(u, c, stage):
        for b in reversed(range(nb)):
            if min(LATER, nb) * (0 if b == last else 1) == stage:
                (t_copy if u % 2 else x_copy)(u // 2, c, b).start()

    def sum_stage(u, c, k):
        reduce_copy(u, c, k).wait_recv()
        size = sizes[k] if k < last else piece
        start = own_at[k + 1] if k < last else own_at[last]
        at = pl.ds(pl.multiple_of(c * cr + start, size), size)
        total = part[u, at, :].astype(jnp.float32) + half[
            u, pl.ds(c * half_rows + half_at[k], size), :
        ].astype(jnp.float32)
        if k < last:
            part[u, at, :] = total.astype(jnp.bfloat16)
            reduce_copy(u, c, k + 1).start()
        else:
            full[u, at, :] = total.astype(jnp.bfloat16)
            if last > 0:
                spread_copy(u, c, last - 1).start()
        start_bulk(u, c, k + 1)

    def spread_stage(u, c, k):
        spread_copy(u, c, k).wait_recv()
        if k > 0:
            spread_copy(u, c, k - 1).start()

    def sum_stages(u, c):
        found = [functools.partial(sum_stage, u, c, k) for k in range(nb)]
        for k in range(last - 1, 0, -1):
            found.append(functools.partial(spread_stage, u, c, k))
        return found

    def finish_sum(u, c):
        if last > 0:
            spread_stage(u, c, 0)

    def begin(l, c):
        at = pl.ds(c * cr, cr)
        u = 2 * l
        x = xbuf[l, at, :]
        mine = rank_in[l, pl.ds(pl.multiple_of(me * width, width), width), :]
        part[u, at, :] = jnp.dot(x, mine, preferred_element_type=jnp.float32).astype(jnp.bfloat16)
        reduce_copy(u, c, 0).start()
        start_bulk(u, c, 0)

    def first(c):
        at = pl.ds(c * cr, cr)
        xbuf[0, at, :] = tokens[at, :]
        begin(0, c)

    def middle(l, c):
        at = pl.ds(c * cr, cr)
        u = 2 * l + 1
        prepare(l, 0)
        finish_sum(u - 1, c)
        for b in range(nb):
            x_copy(l, c, b).wait_recv()
        for j in range(blocks):
            pieces = [xbuf[l, at, pl.ds(j * wb, wb)]]
            for b in range(local_bits):
                pieces.append(xbuf[l, at, pl.ds((j ^ (1 << b)) * wb, wb)])
            for b in range(nb):
                pieces.append(xrecv[l, b, at, pl.ds(j * wb, wb)])
            pieces.append(full[u - 1, at, :])
            pre = jnp.dot(
                jnp.concatenate(pieces, axis=1), wup[l, j], preferred_element_type=jnp.float32
            )
            act = 0.5 * pre * (1.0 + lax.erf(pre * (1.0 / math.sqrt(2.0))))
            hid[at, pl.ds(j * hb, hb)] = act.astype(jnp.bfloat16)
        part[u, at, :] = jnp.dot(
            hid[at, :], rank_down[l], preferred_element_type=jnp.float32
        ).astype(jnp.bfloat16)
        reduce_copy(u, c, 0).start()
        prepare(l, 1)
        own = [None] * blocks
        for j in range(blocks):
            out_j = lax.dot_general(
                hid[at, pl.ds(j * hb, hb)],
                wdown[l, j],
                (((1,), (1,)), ((), ())),
                preferred_element_type=jnp.float32,
            )
            terms = [out_j[:, k * wb : (k + 1) * wb] for k in range(1 + levels)]
            for b in range(nb):
                tsend[l, b, at, pl.ds(j * wb, wb)] = terms[1 + local_bits + b].astype(jnp.bfloat16)
            for to, value in [(j, terms[0])] + [(j ^ (1 << b), terms[1 + b]) for b in range(local_bits)]:
                own[to] = value if own[to] is None else own[to] + value
        start_bulk(u, c, 0)
        for j in range(blocks):
            col = pl.ds(j * wb, wb)
            acc[at, col] = own[j] + xbuf[l, at, col].astype(jnp.float32)

    def close(l, c):
        at = pl.ds(c * cr, cr)
        u = 2 * l + 1
        finish_sum(u, c)
        total = acc[at, :] + jnp.dot(full[u, at, :], rank_out[l], preferred_element_type=jnp.float32)
        for b in range(nb):
            t_copy(l, c, b).wait_recv()
            total = total + trecv[l, b, at, :].astype(jnp.float32)
        result = total.astype(jnp.bfloat16)
        if l + 1 < layers:
            xbuf[l + 1, at, :] = result
            begin(l + 1, c)
        else:
            out[at, :] = result

    plan = []
    for c in range(chunks):
        steps = [functools.partial(first, c)]
        for l in range(layers):
            steps += sum_stages(2 * l, c)
            steps.append(functools.partial(middle, l, c))
            steps += sum_stages(2 * l + 1, c)
            steps.append(functools.partial(close, l, c))
        plan.append(steps)

    plan[0][0]()
    if gather:
        start_weights()
    for tick in range(1, len(plan[0]) + cfg["skew"] * (chunks - 1)):
        for c in range(chunks):
            at = tick - cfg["skew"] * c
            if 0 <= at < len(plan[c]):
                plan[c][at]()

    for l in range(layers):
        if gather:
            for kind in range(2):
                for o in range(1, n_tok):
                    weight_copy(l, kind, o).wait_send()
        for c in range(chunks):
            for b in range(nb):
                x_copy(l, c, b).wait_send()
                t_copy(l, c, b).wait_send()
            for u in (2 * l, 2 * l + 1):
                for k in range(nb):
                    reduce_copy(u, c, k).wait_send()
                for k in range(last):
                    spread_copy(u, c, k).wait_send()


ORDERS = {
    (2, 6): (
        16, 17, 0, 34, 4, 18, 33, 6, 22, 64, 36, 32, 20, 1, 48, 35,
        49, 2, 19, 54, 70, 81, 118, 86, 51, 3, 65, 102, 97, 80, 96, 21,
        134, 113, 129, 67, 52, 66, 50, 112, 150, 128, 144, 160, 176, 82, 98, 145,
        161, 177, 114, 5, 53, 130, 146, 83, 99, 162, 178, 69, 192, 68, 84, 100,
        37, 208, 224, 240, 272, 85, 193, 256, 115, 131, 209, 116, 132, 194, 320, 147,
        179, 148, 164, 225, 241, 289, 257, 273, 101, 304, 210, 180, 336, 352, 226, 117,
        321, 288, 195, 242, 258, 274, 163, 133, 149, 211, 368, 384, 227, 165, 305, 322,
        212, 196, 400, 243, 275, 291, 259, 181, 337, 353, 306, 228, 290, 244, 292, 197,
        276, 338, 260, 323, 432, 369, 385, 307, 213, 354, 401, 433, 308, 229, 370, 339,
        355, 245, 277, 386, 371, 324, 261, 340, 448, 402, 434, 356, 387, 309, 403, 416,
        372, 388, 404, 449, 464, 341, 293, 435, 325, 357, 436, 450, 466, 373, 389, 480,
        496, 465, 405, 451, 421, 420, 467, 483, 419, 482, 417, 452, 418, 468, 481, 437,
        453, 484, 497, 499, 500, 498, 469, 485, 501,
    ),
}
SIZES = {
    1024: (160, 160, 192, 192, 160, 160),
}


def line_order(layers, chunks):
    found = ORDERS.get((layers, chunks))
    if found is not None:
        return [(code // 16 % 16, code // 256, code % 16) for code in found]
    groups = [[3, 4], [5], [6], [7, 8, 9, 10], [11], [12, 13], [14], [15]]
    ticks = [[(step, 0) for step in range(3)]]
    for l in range(layers):
        ticks += [[(step, l) for step in group] for group in groups]
        if l + 1 < layers:
            ticks[-1] += [(step, l + 1) for step in range(3)]
    order = []
    for tick in range(len(ticks) + chunks - 1):
        for c in range(chunks):
            if 0 <= tick - c < len(ticks):
                order += [(step, l, c) for step, l in ticks[tick - c]]
    at = order.index((2, 0, 0)) + 1
    order[at:at] = [(0, 0, chunks), (1, 0, chunks)]
    at = order.index((6, 0, 0)) + 1
    order[at:at] = [(3, 0, chunks), (4, 0, chunks)]
    at = order.index((6, 0, min(1, chunks - 1))) + 1
    order[at:at] = [(5, 0, chunks), (6, 0, chunks), (7, 0, chunks), (8, 0, chunks)]
    at = order.index((11, 0, 0))
    order[at:at] = [(9, 0, chunks)]
    return order


def line_network(cfg, tokens, level_bits, up_in, down_in, rank_in, rank_up, rank_down, rank_out, out, *scratch):
    (xbuf, xrecv, tsend, trecv, terms_to, part, got, full, hid, acc, wup, wdown, outs) = scratch[:13]
    rest = scratch[13:]
    layers, rows, width = cfg["layers"], cfg["rows"], cfg["width"]
    blocks, wb, hb = cfg["blocks"], cfg["wb"], cfg["hb"]
    n_tok, rank, sizes = cfg["n_tok"], cfg["rank"], cfg["sizes"]
    chunks = len(sizes)
    starts = [sum(sizes[:c]) for c in range(chunks)]
    local_bits = bits_of(blocks)
    nb = 3
    levels = local_bits + nb
    upg, downg = rest[:layers], rest[layers : 2 * layers]
    wsend, wrecv, wloc, osend, orecv, qsend, qrecv = rest[2 * layers : 2 * layers + 7]
    xs_sem, xr_sem, ts_sem, tr_sem, as_sem, ar_sem = rest[2 * layers + 7 :]

    me = lax.axis_index("feat")
    me_tok = lax.axis_index("tok")
    bit = [(me // (1 << b)) % 2 for b in range(nb)]
    flip = [(1 << b) * (1 - 2 * bit[b]) for b in range(nb)]
    across, near, far = [me + flip[b] for b in range(nb)]
    cross = me + flip[1] + flip[2]
    is_inner = bit[1] + bit[2] == 1
    is_outer = bit[1] + bit[2] != 1
    core_peer = me_tok + 1 - 2 * (me_tok % 2)
    chip_peer = me_tok + 2 - 4 * ((me_tok // 2) % 2)

    def inner(f):
        pl.when(is_inner)(f)

    def outer(f):
        pl.when(is_outer)(f)

    barrier = pltpu.get_barrier_semaphore()
    for to in (across, near):
        pl.semaphore_signal(barrier, inc=1, device_id={"feat": to}, device_id_type=MESH)
    for to in (core_peer, chip_peer):
        pl.semaphore_signal(barrier, inc=1, device_id={"tok": to}, device_id_type=MESH)

    @inner
    def _():
        pl.semaphore_signal(barrier, inc=1, device_id={"feat": cross}, device_id_type=MESH)
        pl.semaphore_wait(barrier, 5)

    @outer
    def _():
        pl.semaphore_wait(barrier, 4)

    def remote(src, dst, send, recv, axis, to):
        return pltpu.make_async_remote_copy(
            src_ref=src, dst_ref=dst, send_sem=send, recv_sem=recv, device_id={axis: to}, device_id_type=MESH
        )

    up_cols, down_cols = up_in.shape[-1], down_in.shape[-2]

    def shard(l, kind, owner):
        if kind == 0:
            return upg[l].at[:, :, :, pl.ds(pl.multiple_of(owner * up_cols, up_cols), up_cols)]
        return downg[l].at[:, :, pl.ds(pl.multiple_of(owner * down_cols, down_cols), down_cols), :]

    def weight_copy(l, kind, way):
        src = (up_in if kind == 0 else down_in).at[l]
        if way == 0:
            return pltpu.make_async_copy(src, shard(l, kind, me_tok), wloc.at[l, kind])
        if way == 1:
            to, at = chip_peer, shard(l, kind, me_tok)
        elif way == 2:
            to, at = core_peer, shard(l, kind, me_tok)
        else:
            src = at = shard(l, kind, chip_peer)
            to = core_peer
        return remote(src, at, wsend.at[l, kind, way - 1], wrecv.at[l, kind, way - 1], "tok", to)

    def start_weights(l):
        for kind in range(2):
            for way in range(3):
                weight_copy(l, kind, way).start()

    shared = set()

    def share_weights(l, kind):
        if (l, kind) in shared:
            return
        shared.add((l, kind))
        weight_copy(l, kind, 1).wait_recv()
        weight_copy(l, kind, 3).start()

    quarter = rank // n_tok

    def out_rows(slot, owner):
        at = pl.ds(pl.multiple_of(owner * quarter, quarter), quarter)
        return outs.at[:, :, at, :] if slot is None else outs.at[slot, :, at, :]

    def share_copy(way):
        at = out_rows(None, chip_peer if way == 2 else me_tok)
        return remote(at, at, qsend.at[way], qrecv.at[way], "tok", core_peer if way else chip_peer)

    def share_outs():
        share_copy(0).wait_recv()
        share_copy(2).start()

    prepared = set()

    def prepare(l, kind):
        if (l, kind) in prepared:
            return
        prepared.add((l, kind))
        share_weights(l, kind)
        weight_copy(l, kind, 0).wait()
        weight_copy(l, kind, 2).wait_recv()
        weight_copy(l, kind, 3).wait_recv()
        order = []
        for b in range(levels):
            at = 0
            for k in range(levels):
                at = jnp.maximum(at, jnp.where(level_bits[l, k] == b, 1 + k, 0))
            order.append(at)
        for j in range(blocks):
            if kind == 0:
                wup[l, j, pl.ds(0, wb), :] = upg[l][j, 0]
                for b in range(levels):
                    wup[l, j, pl.ds((1 + b) * wb, wb), :] = upg[l][j, order[b]]
                wup[l, j, pl.ds((1 + levels) * wb, rank), :] = rank_up[l, :, pl.ds(j * hb, hb)]
            else:
                wdown[l, j, pl.ds(0, wb), :] = downg[l][j, 0]
                for b in range(levels):
                    wdown[l, j, pl.ds((1 + b) * wb, wb), :] = downg[l][j, order[b]]

    def rows_of(c):
        return pl.ds(starts[c], sizes[c])

    def own_x(l):
        return xbuf.at[l] if l else tokens

    WAYS = (("own", 0, across), ("own", 1, near), ("own", 3, cross), (1, 2, cross), (3, 2, near), (2, 3, near))

    def x_copy(l, c, way):
        src, slot, to = WAYS[way]
        if c == chunks:
            at = pl.ds(pl.multiple_of(me_tok * quarter, quarter), quarter)
            src = rank_out.at[:, at, :] if src == "own" else out_rows(src - 1, me_tok)
            return remote(src, out_rows(slot - 1, me_tok), osend.at[way], orecv.at[slot], "feat", to)
        at = rows_of(c)
        src = own_x(l).at[at, :] if src == "own" else xrecv.at[l, src, at, :]
        return remote(src, xrecv.at[l, slot, at, :], xs_sem.at[l, c, way], xr_sem.at[l, c, slot], "feat", to)

    T_WAYS = ((0, 0, across), (1, 1, near), (2, 2, near), (3, 3, near), (2, 4, cross), (3, 5, cross))

    def t_copy(l, c, way):
        src, slot, to = T_WAYS[way]
        at = rows_of(c)
        return remote(
            tsend.at[l, src, at, :], trecv.at[l, slot, at, :], ts_sem.at[l, c, way], tr_sem.at[l, c, slot], "feat", to
        )

    def pair_copy(u, c):
        at = rows_of(c)
        return remote(part.at[u, at, :], got.at[u, at, :], as_sem.at[u, c], ar_sem.at[u, c], "feat", across)

    def pair_sum(u, c):
        pair_copy(u, c).wait_recv()
        at = rows_of(c)
        total = part[u, at, :].astype(jnp.float32) + got[u, at, :].astype(jnp.float32)
        full[u, at, :] = total.astype(jnp.bfloat16)

    def send_cross(l, c):
        @inner
        def _():
            x_copy(l, c, 2).start()

    def send_near(l, c):
        x_copy(l, c, 1).start()

    def send_across(l, c):
        x_copy(l, c, 0).start()

    def relay_in(l, c):
        x_copy(l, c, 1).wait_recv()

        @inner
        def _():
            x_copy(l, c, 3).start()

    def relay_cross(l, c):
        @inner
        def _():
            x_copy(l, c, 2).wait_recv()
            x_copy(l, c, 4).start()

    def relay_out(l, c):
        @inner
        def _():
            x_copy(l, c, 3).wait_recv()
            x_copy(l, c, 5).start()

    def line_done(l, c):
        @outer
        def _():
            x_copy(l, c, 4).wait_recv()
            x_copy(l, c, 5).wait_recv()

    def begin(l, c):
        line_done(l, c)
        if c == chunks:
            share_copy(0).start()
            share_copy(1).start()
            return
        at = rows_of(c)
        total = None
        for slot, owner in ((0, me), (1, near), (2, far), (3, cross)):
            x = xrecv[l, slot, at, :] if slot else own_x(l)[at, :]
            term = jnp.dot(
                x, rank_in[l, pl.ds(pl.multiple_of(owner * width, width), width), :],
                preferred_element_type=jnp.float32,
            )
            total = term if total is None else total + term
        part[2 * l, at, :] = total.astype(jnp.bfloat16)
        pair_copy(2 * l, c).start()

    def latent(l, c):
        if c == chunks:
            return share_weights(0, 0)
        pair_sum(2 * l, c)

    def up(l, c):
        if c == chunks:
            return share_weights(0, 1)
        at = rows_of(c)
        xin = own_x(l)
        prepare(l, 0)
        x_copy(l, c, 0).wait_recv()
        for j in range(blocks):
            pieces = [xin[at, pl.ds(j * wb, wb)]]
            for b in range(local_bits):
                pieces.append(xin[at, pl.ds((j ^ (1 << b)) * wb, wb)])
            for b in range(nb):
                pieces.append(xrecv[l, b, at, pl.ds(j * wb, wb)])
            pieces.append(full[2 * l, at, :])
            pre = jnp.dot(
                jnp.concatenate(pieces, axis=1), wup[l, j], preferred_element_type=jnp.float32
            )
            act = 0.5 * pre * (1.0 + lax.erf(pre * (1.0 / math.sqrt(2.0))))
            hid[at, pl.ds(j * hb, hb)] = act.astype(jnp.bfloat16)
        part[2 * l + 1, at, :] = jnp.dot(
            hid[at, :], rank_down[l], preferred_element_type=jnp.float32
        ).astype(jnp.bfloat16)
        pair_copy(2 * l + 1, c).start()

    def down(l, c):
        if c == chunks:
            return share_outs()
        at = rows_of(c)
        xin = own_x(l)
        prepare(l, 1)
        own = [None] * blocks
        for j in range(blocks):
            col = pl.ds(j * wb, wb)
            out_j = lax.dot_general(
                hid[at, pl.ds(j * hb, hb)],
                wdown[l, j],
                (((1,), (1,)), ((), ())),
                preferred_element_type=jnp.float32,
            )
            terms = [out_j[:, k * wb : (k + 1) * wb] for k in range(1 + levels)]
            tsend[l, 0, at, col] = terms[1 + local_bits].astype(jnp.bfloat16)
            for b in range(1, nb):
                terms_to[b - 1, at, col] = terms[1 + local_bits + b]
            for to, value in [(j, terms[0])] + [(j ^ (1 << b), terms[1 + b]) for b in range(local_bits)]:
                own[to] = value if own[to] is None else own[to] + value
        for j in range(blocks):
            col = pl.ds(j * wb, wb)
            acc[at, col] = own[j] + xin[at, col].astype(jnp.float32)

    def send_t_across(l, c):
        t_copy(l, c, 0).start()

    outs_ready = set()

    def low_rank(l, c):
        if not outs_ready:
            outs_ready.add(0)
            share_copy(1).wait_recv()
            share_copy(2).wait_recv()
        at = rows_of(c)
        pair_sum(2 * l + 1, c)
        low = full[2 * l + 1, at, :]

        def term(slot):
            return jnp.dot(low, outs[slot - 1, l], preferred_element_type=jnp.float32)

        @inner
        def _():
            for slot in (1, 2):
                terms_to[slot - 1, at, :] += term(slot)
            terms_to[2, at, :] = term(3)

        @outer
        def _():
            tsend[l, 3, at, :] = term(3).astype(jnp.bfloat16)
            t_copy(l, c, 3).start()
            for slot in (2, 1):
                tsend[l, slot, at, :] = (terms_to[slot - 1, at, :] + term(slot)).astype(jnp.bfloat16)
                t_copy(l, c, slot).start()

        acc[at, :] += jnp.dot(low, rank_out[l], preferred_element_type=jnp.float32)

    def pass_on(l, c, slot, way):
        at = rows_of(c)

        @inner
        def _():
            t_copy(l, c, {3: 3, 2: 2, 4: 4}[slot]).wait_recv()
            src = T_WAYS[way][0]
            total = terms_to[src - 1, at, :] + trecv[l, slot, at, :].astype(jnp.float32)
            tsend[l, src, at, :] = total.astype(jnp.bfloat16)
            t_copy(l, c, way).start()

    def pass_far(l, c):
        pass_on(l, c, 3, 4)

    def pass_cross(l, c):
        pass_on(l, c, 2, 5)

    def pass_out(l, c):
        pass_on(l, c, 4, 1)

    def close(l, c):
        at = rows_of(c)

        @inner
        def _():
            t_copy(l, c, 5).wait_recv()
            acc[at, :] += trecv[l, 5, at, :].astype(jnp.float32)

        t_copy(l, c, 0).wait_recv()
        t_copy(l, c, 1).wait_recv()
        total = acc[at, :]
        for slot in range(2):
            total = total + trecv[l, slot, at, :].astype(jnp.float32)
        result = total.astype(jnp.bfloat16)
        if l + 1 < layers:
            xbuf[l + 1, at, :] = result
        else:
            out[at, :] = result

    steps = [
        send_cross, send_near, send_across, relay_in, relay_cross, relay_out, begin, latent, up, down,
        send_t_across, low_rank, pass_far, pass_cross, pass_out, close,
    ]
    weights_left = list(range(layers))
    for at, (step, l, c) in enumerate(line_order(layers, chunks)):
        steps[step](l, c)
        if at == 2:
            start_weights(weights_left.pop(0))
        if (step, c) == (9, chunks):
            while weights_left:
                start_weights(weights_left.pop(0))

    for l in range(layers):
        for kind in range(2):
            for way in range(1, 4):
                weight_copy(l, kind, way).wait_send()
        for c in range(chunks + (l == 0)):
            x_copy(l, c, 1).wait_send()

            @inner
            def _():
                for way in range(2, 6):
                    x_copy(l, c, way).wait_send()

            if c == chunks:
                continue
            x_copy(l, c, 0).wait_send()
            for way in range(2):
                t_copy(l, c, way).wait_send()

            @inner
            def _():
                for way in (4, 5):
                    t_copy(l, c, way).wait_send()

            @outer
            def _():
                for way in (2, 3):
                    t_copy(l, c, way).wait_send()

            for u in (2 * l, 2 * l + 1):
                pair_copy(u, c).wait_send()
    for way in range(3):
        share_copy(way).wait_send()


def per_device(tokens, level_bits, up_blocks, down_blocks, rank_in, rank_up, rank_down, rank_out):
    rows, width = tokens.shape
    layers, blocks, parts, wb, up_cols = up_blocks.shape
    hb, down_cols = down_blocks.shape[3:]
    n_tok, n_feat = lax.axis_size("tok"), lax.axis_size("feat")
    rank = rank_in.shape[-1]
    hidden = blocks * hb
    nb = bits_of(n_feat)
    chunk = min(CHUNK_ROWS, rows)
    chunks = rows // chunk
    gather = n_tok > 1 and up_cols % 128 == 0 and down_cols % 16 == 0
    if not gather:
        up_blocks = lax.all_gather(up_blocks, "tok", axis=4, tiled=True)
        down_blocks = lax.all_gather(down_blocks, "tok", axis=4, tiled=True)
    down_blocks = jnp.swapaxes(down_blocks, 3, 4)
    cfg = dict(
        layers=layers, rows=rows, width=width, blocks=blocks, wb=wb, hb=hb, n_feat=n_feat,
        n_tok=n_tok, rank=rank, chunk=chunk, gather=gather, skew=SKEW,
    )
    bf16 = jnp.bfloat16
    uses = 2 * layers
    half_rows = chunk
    scratch = [
        pltpu.VMEM((layers, rows, width), bf16),
        pltpu.VMEM((layers, nb, rows, width), bf16),
        pltpu.VMEM((layers, nb, rows, width), bf16),
        pltpu.VMEM((layers, nb, rows, width), bf16),
        pltpu.VMEM((uses, rows, rank), bf16),
        pltpu.VMEM((uses, chunks * half_rows, rank), bf16),
        pltpu.VMEM((uses, rows, rank), bf16),
        pltpu.VMEM((rows, hidden), bf16),
        pltpu.VMEM((rows, width), jnp.float32),
        pltpu.VMEM((layers, blocks, parts * wb + rank, hb), bf16),
        pltpu.VMEM((layers, blocks, parts * wb, hb), bf16),
    ]
    dma = pltpu.SemaphoreType.DMA
    line = gather and nb == 3 and n_tok == 4 and rank % (16 * n_tok) == 0 and rows % LINE_CHUNK == 0
    if line:
        sizes = SIZES.get(rows) or (LINE_CHUNK,) * (rows // LINE_CHUNK)
        cfg["sizes"] = sizes
        pieces = len(sizes)
        scratch[1:5] = [
            pltpu.VMEM((layers, nb + 1, rows, width), bf16),
            pltpu.VMEM((layers, nb + 1, rows, width), bf16),
            pltpu.VMEM((layers, 2 * nb, rows, width), bf16),
            pltpu.VMEM((nb, rows, width), jnp.float32),
            pltpu.VMEM((uses, rows, rank), bf16),
        ]
        scratch[6] = pltpu.VMEM((uses, rows, rank), bf16)
        scratch += [pltpu.VMEM((nb, layers, rank, width), bf16)]
        scratch += [pltpu.VMEM((blocks, parts, wb, hb), bf16)] * (2 * layers)
        scratch += [dma((layers, 2, 3)), dma((layers, 2, 3)), dma((layers, 2)), dma((6,)), dma((4,)), dma((3,)), dma((3,))]
        scratch += [dma((layers, pieces, 6)), dma((layers, pieces, 4)), dma((layers, pieces, 6)), dma((layers, pieces, 6))]
        scratch += [dma((uses, pieces))] * 2
    elif gather:
        scratch += [pltpu.VMEM((blocks, parts, wb, hb), bf16)] * (2 * layers)
        scratch += [
            dma((layers, 2, n_tok - 1)),
            dma((layers, 2, n_tok - 1)),
            dma((layers, 2)),
        ]
    if not line:
        scratch += [dma((layers, chunks, nb))] * 4 + [dma((uses, chunks, 2 * nb - 1))] * 2
    vmem = pl.BlockSpec(memory_space=pltpu.VMEM)
    smem = pl.BlockSpec(memory_space=pltpu.SMEM)
    return pl.pallas_call(
        functools.partial(line_network if line else network, cfg),
        out_shape=jax.ShapeDtypeStruct((rows, width), bf16),
        in_specs=[vmem, smem] + [vmem] * 6,
        out_specs=vmem,
        scratch_shapes=scratch,
        compiler_params=pltpu.CompilerParams(
            collective_id=0, has_side_effects=True, vmem_limit_bytes=63 * 1024 * 1024
        ),
    )(tokens, level_bits, up_blocks, down_blocks, rank_in, rank_up, rank_down, rank_out)


def solution(mesh):
    return jax.shard_map(
        per_device,
        mesh=mesh,
        in_specs=(
            P("tok", "feat"),
            P(),
            P(None, "feat", None, None, "tok"),
            P(None, "feat", None, None, "tok"),
            P(),
            P(None, None, "feat"),
            P(None, "feat", None),
            P(None, None, "feat"),
        ),
        out_specs=P("tok", "feat"),
        check_vma=False,
    )
```

```python
import functools
import math

import jax
import jax.numpy as jnp
from jax import lax
from jax.experimental import pallas as pl
from jax.experimental.pallas import tpu as pltpu
from jax.sharding import PartitionSpec as P

CHUNK_ROWS = 256
LINE_CHUNK = 128
SKEW = 1
LATER = 1
MESH = pl.DeviceIdType.MESH


def bits_of(count):
    return count.bit_length() - 1


def network(cfg, tokens, level_bits, up_in, down_in, rank_in, rank_up, rank_down, rank_out, out, *scratch):
    (xbuf, xrecv, tsend, trecv, part, half, full, hid, acc, wup, wdown) = scratch[:11]
    rest = scratch[11:]
    layers, rows, width = cfg["layers"], cfg["rows"], cfg["width"]
    blocks, wb, hb = cfg["blocks"], cfg["wb"], cfg["hb"]
    n_feat, n_tok, rank = cfg["n_feat"], cfg["n_tok"], cfg["rank"]
    cr = cfg["chunk"]
    chunks = rows // cr
    local_bits = bits_of(blocks)
    nb = bits_of(n_feat)
    levels = local_bits + nb
    gather = cfg["gather"]
    if gather:
        upg, downg = rest[:layers], rest[layers : 2 * layers]
        wsend, wrecv, wloc = rest[2 * layers : 2 * layers + 3]
        rest = rest[2 * layers + 3 :]
    else:
        upg = [up_in.at[l] for l in range(layers)]
        downg = [down_in.at[l] for l in range(layers)]
    xs_sem, xr_sem, ts_sem, tr_sem, as_sem, ar_sem = rest

    me = lax.axis_index("feat")
    me_tok = lax.axis_index("tok")
    mybit = [(me // (1 << b)) % 2 for b in range(nb)]
    partner = [me + (1 << b) * (1 - 2 * mybit[b]) for b in range(nb)]

    barrier = pltpu.get_barrier_semaphore()
    for b in range(nb):
        pl.semaphore_signal(barrier, inc=1, device_id={"feat": partner[b]}, device_id_type=MESH)
    greeted = nb
    if gather:
        for o in range(1, n_tok):
            pl.semaphore_signal(
                barrier, inc=1, device_id={"tok": lax.rem(me_tok + o, n_tok)}, device_id_type=MESH
            )
        greeted += n_tok - 1
    pl.semaphore_wait(barrier, greeted)

    def weight_copy(l, kind, o):
        if kind == 0:
            cols = up_in.shape[-1]
            src = up_in.at[l]
            dst = upg[l].at[:, :, :, pl.ds(pl.multiple_of(me_tok * cols, cols), cols)]
        else:
            cols = down_in.shape[-2]
            src = down_in.at[l]
            dst = downg[l].at[:, :, pl.ds(pl.multiple_of(me_tok * cols, cols), cols), :]
        if o == 0:
            return pltpu.make_async_copy(src, dst, wloc.at[l, kind])
        return pltpu.make_async_remote_copy(
            src_ref=src,
            dst_ref=dst,
            send_sem=wsend.at[l, kind, o - 1],
            recv_sem=wrecv.at[l, kind, o - 1],
            device_id={"tok": lax.rem(me_tok + o, n_tok)},
            device_id_type=MESH,
        )

    def start_weights():
        for l in range(layers):
            for kind in range(2):
                for o in range(n_tok):
                    weight_copy(l, kind, o).start()

    prepared = set()

    def prepare(l, kind):
        if (l, kind) in prepared:
            return
        prepared.add((l, kind))
        if gather:
            for o in range(n_tok):
                copy = weight_copy(l, kind, o)
                copy.wait() if o == 0 else copy.wait_recv()
        order = []
        for b in range(levels):
            at = 0
            for k in range(levels):
                at = jnp.maximum(at, jnp.where(level_bits[l, k] == b, 1 + k, 0))
            order.append(at)
        for j in range(blocks):
            if kind == 0:
                wup[l, j, pl.ds(0, wb), :] = upg[l][j, 0]
                for b in range(levels):
                    wup[l, j, pl.ds((1 + b) * wb, wb), :] = upg[l][j, order[b]]
                wup[l, j, pl.ds((1 + levels) * wb, rank), :] = rank_up[l, :, pl.ds(j * hb, hb)]
            else:
                wdown[l, j, pl.ds(0, wb), :] = downg[l][j, 0]
                for b in range(levels):
                    wdown[l, j, pl.ds((1 + b) * wb, wb), :] = downg[l][j, order[b]]

    def x_copy(l, c, b):
        at = pl.ds(c * cr, cr)
        return pltpu.make_async_remote_copy(
            src_ref=xbuf.at[l, at, :],
            dst_ref=xrecv.at[l, b, at, :],
            send_sem=xs_sem.at[l, c, b],
            recv_sem=xr_sem.at[l, c, b],
            device_id={"feat": partner[b]},
            device_id_type=MESH,
        )

    def t_copy(l, c, b):
        at = pl.ds(c * cr, cr)
        return pltpu.make_async_remote_copy(
            src_ref=tsend.at[l, b, at, :],
            dst_ref=trecv.at[l, b, at, :],
            send_sem=ts_sem.at[l, c, b],
            recv_sem=tr_sem.at[l, c, b],
            device_id={"feat": partner[b]},
            device_id_type=MESH,
        )

    last = nb - 1
    sizes = [cr >> (k + 1) for k in range(last)]
    own_at = [0]
    for k in range(last):
        own_at.append(own_at[-1] + mybit[k] * sizes[k])
    away_at = [own_at[k] + (1 - mybit[k]) * sizes[k] for k in range(last)]
    piece = cr >> last
    half_at = [sum(sizes[:k]) for k in range(last + 1)]
    half_rows = half_at[-1] + piece

    def reduce_copy(u, c, k):
        if k < last:
            src = part.at[u, pl.ds(pl.multiple_of(c * cr + away_at[k], sizes[k]), sizes[k]), :]
            size = sizes[k]
        else:
            src = part.at[u, pl.ds(pl.multiple_of(c * cr + own_at[last], piece), piece), :]
            size = piece
        return pltpu.make_async_remote_copy(
            src_ref=src,
            dst_ref=half.at[u, pl.ds(c * half_rows + half_at[k], size), :],
            send_sem=as_sem.at[u, c, k],
            recv_sem=ar_sem.at[u, c, k],
            device_id={"feat": partner[k]},
            device_id_type=MESH,
        )

    def spread_copy(u, c, k):
        size = cr >> (k + 1)
        at = pl.ds(pl.multiple_of(c * cr + own_at[k + 1], size), size)
        return pltpu.make_async_remote_copy(
            src_ref=full.at[u, at, :],
            dst_ref=full.at[u, at, :],
            send_sem=as_sem.at[u, c, nb + k],
            recv_sem=ar_sem.at[u, c, nb + k],
            device_id={"feat": partner[k]},
            device_id_type=MESH,
        )

    def start_bulk(u, c, stage):
        for b in reversed(range(nb)):
            if min(LATER, nb) * (0 if b == last else 1) == stage:
                (t_copy if u % 2 else x_copy)(u // 2, c, b).start()

    def sum_stage(u, c, k):
        reduce_copy(u, c, k).wait_recv()
        size = sizes[k] if k < last else piece
        start = own_at[k + 1] if k < last else own_at[last]
        at = pl.ds(pl.multiple_of(c * cr + start, size), size)
        total = part[u, at, :].astype(jnp.float32) + half[
            u, pl.ds(c * half_rows + half_at[k], size), :
        ].astype(jnp.float32)
        if k < last:
            part[u, at, :] = total.astype(jnp.bfloat16)
            reduce_copy(u, c, k + 1).start()
        else:
            full[u, at, :] = total.astype(jnp.bfloat16)
            if last > 0:
                spread_copy(u, c, last - 1).start()
        start_bulk(u, c, k + 1)

    def spread_stage(u, c, k):
        spread_copy(u, c, k).wait_recv()
        if k > 0:
            spread_copy(u, c, k - 1).start()

    def sum_stages(u, c):
        found = [functools.partial(sum_stage, u, c, k) for k in range(nb)]
        for k in range(last - 1, 0, -1):
            found.append(functools.partial(spread_stage, u, c, k))
        return found

    def finish_sum(u, c):
        if last > 0:
            spread_stage(u, c, 0)

    def begin(l, c):
        at = pl.ds(c * cr, cr)
        u = 2 * l
        x = xbuf[l, at, :]
        mine = rank_in[l, pl.ds(pl.multiple_of(me * width, width), width), :]
        part[u, at, :] = jnp.dot(x, mine, preferred_element_type=jnp.float32).astype(jnp.bfloat16)
        reduce_copy(u, c, 0).start()
        start_bulk(u, c, 0)

    def first(c):
        at = pl.ds(c * cr, cr)
        xbuf[0, at, :] = tokens[at, :]
        begin(0, c)

    def middle(l, c):
        at = pl.ds(c * cr, cr)
        u = 2 * l + 1
        prepare(l, 0)
        finish_sum(u - 1, c)
        for b in range(nb):
            x_copy(l, c, b).wait_recv()
        for j in range(blocks):
            pieces = [xbuf[l, at, pl.ds(j * wb, wb)]]
            for b in range(local_bits):
                pieces.append(xbuf[l, at, pl.ds((j ^ (1 << b)) * wb, wb)])
            for b in range(nb):
                pieces.append(xrecv[l, b, at, pl.ds(j * wb, wb)])
            pieces.append(full[u - 1, at, :])
            pre = jnp.dot(
                jnp.concatenate(pieces, axis=1), wup[l, j], preferred_element_type=jnp.float32
            )
            act = 0.5 * pre * (1.0 + lax.erf(pre * (1.0 / math.sqrt(2.0))))
            hid[at, pl.ds(j * hb, hb)] = act.astype(jnp.bfloat16)
        part[u, at, :] = jnp.dot(
            hid[at, :], rank_down[l], preferred_element_type=jnp.float32
        ).astype(jnp.bfloat16)
        reduce_copy(u, c, 0).start()
        prepare(l, 1)
        own = [None] * blocks
        for j in range(blocks):
            out_j = lax.dot_general(
                hid[at, pl.ds(j * hb, hb)],
                wdown[l, j],
                (((1,), (1,)), ((), ())),
                preferred_element_type=jnp.float32,
            )
            terms = [out_j[:, k * wb : (k + 1) * wb] for k in range(1 + levels)]
            for b in range(nb):
                tsend[l, b, at, pl.ds(j * wb, wb)] = terms[1 + local_bits + b].astype(jnp.bfloat16)
            for to, value in [(j, terms[0])] + [(j ^ (1 << b), terms[1 + b]) for b in range(local_bits)]:
                own[to] = value if own[to] is None else own[to] + value
        start_bulk(u, c, 0)
        for j in range(blocks):
            col = pl.ds(j * wb, wb)
            acc[at, col] = own[j] + xbuf[l, at, col].astype(jnp.float32)

    def close(l, c):
        at = pl.ds(c * cr, cr)
        u = 2 * l + 1
        finish_sum(u, c)
        total = acc[at, :] + jnp.dot(full[u, at, :], rank_out[l], preferred_element_type=jnp.float32)
        for b in range(nb):
            t_copy(l, c, b).wait_recv()
            total = total + trecv[l, b, at, :].astype(jnp.float32)
        result = total.astype(jnp.bfloat16)
        if l + 1 < layers:
            xbuf[l + 1, at, :] = result
            begin(l + 1, c)
        else:
            out[at, :] = result

    plan = []
    for c in range(chunks):
        steps = [functools.partial(first, c)]
        for l in range(layers):
            steps += sum_stages(2 * l, c)
            steps.append(functools.partial(middle, l, c))
            steps += sum_stages(2 * l + 1, c)
            steps.append(functools.partial(close, l, c))
        plan.append(steps)

    plan[0][0]()
    if gather:
        start_weights()
    for tick in range(1, len(plan[0]) + cfg["skew"] * (chunks - 1)):
        for c in range(chunks):
            at = tick - cfg["skew"] * c
            if 0 <= at < len(plan[c]):
                plan[c][at]()

    for l in range(layers):
        if gather:
            for kind in range(2):
                for o in range(1, n_tok):
                    weight_copy(l, kind, o).wait_send()
        for c in range(chunks):
            for b in range(nb):
                x_copy(l, c, b).wait_send()
                t_copy(l, c, b).wait_send()
            for u in (2 * l, 2 * l + 1):
                for k in range(nb):
                    reduce_copy(u, c, k).wait_send()
                for k in range(last):
                    spread_copy(u, c, k).wait_send()


ORDERS = {
    (2, 7): (
        34, 22, 35, 16, 1, 7, 23, 3, 17, 2, 0, 37, 19, 48, 32, 18,
        49, 65, 33, 55, 71, 64, 38, 6, 36, 80, 119, 87, 96, 51, 103, 20,
        81, 97, 50, 66, 112, 135, 128, 54, 113, 129, 21, 151, 82, 98, 4, 144,
        176, 160, 145, 177, 86, 114, 161, 130, 83, 52, 67, 99, 70, 53, 146, 102,
        192, 84, 68, 208, 178, 100, 115, 131, 209, 224, 193, 240, 272, 5, 116, 147,
        163, 132, 179, 256, 85, 162, 225, 241, 273, 257, 210, 69, 101, 148, 289, 194,
        321, 180, 226, 242, 195, 304, 274, 117, 320, 211, 133, 149, 165, 305, 164, 336,
        352, 227, 196, 288, 181, 243, 275, 212, 258, 118, 134, 337, 353, 306, 368, 228,
        259, 290, 244, 292, 322, 276, 150, 166, 182, 197, 213, 260, 338, 369, 385, 384,
        354, 229, 323, 291, 245, 277, 293, 308, 307, 401, 433, 198, 400, 432, 340, 324,
        339, 214, 370, 386, 402, 309, 356, 230, 246, 262, 278, 355, 465, 261, 434, 372,
        388, 326, 404, 416, 449, 325, 371, 387, 436, 310, 294, 341, 450, 481, 357, 342,
        358, 466, 448, 403, 435, 373, 374, 390, 406, 452, 420, 468, 389, 405, 484, 438,
        421, 464, 451, 418, 483, 422, 467, 470, 454, 480, 500, 482, 437, 453, 419, 496,
        417, 486, 469, 502, 485, 499, 498, 497, 501,
    ),
}
SIZES = {
    1024: (128, 128, 160, 160, 160, 160, 128),
}


def line_order(layers, chunks):
    found = ORDERS.get((layers, chunks))
    if found is not None:
        return [(code // 16 % 16, code // 256, code % 16) for code in found]
    groups = [[3, 4], [5], [6], [7, 8, 9, 10], [11], [12, 13], [14], [15]]
    ticks = [[(step, 0) for step in range(3)]]
    for l in range(layers):
        ticks += [[(step, l) for step in group] for group in groups]
        if l + 1 < layers:
            ticks[-1] += [(step, l + 1) for step in range(3)]
    order = []
    for tick in range(len(ticks) + chunks - 1):
        for c in range(chunks):
            if 0 <= tick - c < len(ticks):
                order += [(step, l, c) for step, l in ticks[tick - c]]
    at = order.index((2, 0, 0)) + 1
    order[at:at] = [(0, 0, chunks), (1, 0, chunks)]
    at = order.index((6, 0, 0)) + 1
    order[at:at] = [(3, 0, chunks), (4, 0, chunks)]
    at = order.index((6, 0, min(1, chunks - 1))) + 1
    order[at:at] = [(5, 0, chunks), (6, 0, chunks), (7, 0, chunks), (8, 0, chunks)]
    at = order.index((11, 0, 0))
    order[at:at] = [(9, 0, chunks)]
    return order


def line_network(cfg, tokens, level_bits, up_in, down_in, all_in, all_up, all_down, all_out, out, *scratch):
    (xbuf, xrecv, tsend, trecv, terms_to, part, got, full, hid, acc, wup, wdown, outs) = scratch[:13]
    rank_in, rank_down, rank_out, load_sem = scratch[13:17]
    rest = scratch[17:]
    layers, rows, width = cfg["layers"], cfg["rows"], cfg["width"]
    blocks, wb, hb = cfg["blocks"], cfg["wb"], cfg["hb"]
    n_tok, rank, sizes = cfg["n_tok"], cfg["rank"], cfg["sizes"]
    chunks = len(sizes)
    starts = [sum(sizes[:c]) for c in range(chunks)]
    local_bits = bits_of(blocks)
    nb = 3
    levels = local_bits + nb
    upg, downg = rest[:layers], rest[layers : 2 * layers]
    wsend, wrecv, wloc, osend, orecv, qsend, qrecv = rest[2 * layers : 2 * layers + 7]
    xs_sem, xr_sem, ts_sem, tr_sem, as_sem, ar_sem = rest[2 * layers + 7 :]

    me = lax.axis_index("feat")
    me_tok = lax.axis_index("tok")
    bit = [(me // (1 << b)) % 2 for b in range(nb)]
    flip = [(1 << b) * (1 - 2 * bit[b]) for b in range(nb)]
    across, near, far = [me + flip[b] for b in range(nb)]
    cross = me + flip[1] + flip[2]
    is_inner = bit[1] + bit[2] == 1
    is_outer = bit[1] + bit[2] != 1
    core_peer = me_tok + 1 - 2 * (me_tok % 2)
    chip_peer = me_tok + 2 - 4 * ((me_tok // 2) % 2)

    def inner(f):
        pl.when(is_inner)(f)

    def outer(f):
        pl.when(is_outer)(f)

    low = (1 + levels) * wb
    loads = {"x": [(tokens, xbuf.at[0])], "in": [(all_in, rank_in)]}
    for l in range(layers):
        loads["up", l] = [
            (all_up.at[l, :, pl.ds(j * hb, hb)], wup.at[l, j, pl.ds(low, rank), :]) for j in range(blocks)
        ]
    loads["down"] = [(all_down, rank_down)]
    loads["out"] = [(all_out, rank_out)]
    pending, count = {}, 0
    for name, pairs in loads.items():
        pending[name] = []
        for src, dst in pairs:
            pending[name].append(pltpu.make_async_copy(src, dst, load_sem.at[count]))
            count += 1

    def loaded(*names):
        for name in names:
            for copy in pending.pop(name, ()):
                copy.wait()

    barrier = pltpu.get_barrier_semaphore()
    for to in (across, near):
        pl.semaphore_signal(barrier, inc=1, device_id={"feat": to}, device_id_type=MESH)
    for to in (core_peer, chip_peer):
        pl.semaphore_signal(barrier, inc=1, device_id={"tok": to}, device_id_type=MESH)

    for name in pending:
        for copy in pending[name]:
            copy.start()

    @inner
    def _():
        pl.semaphore_signal(barrier, inc=1, device_id={"feat": cross}, device_id_type=MESH)
        pl.semaphore_wait(barrier, 5)

    @outer
    def _():
        pl.semaphore_wait(barrier, 4)

    def remote(src, dst, send, recv, axis, to):
        return pltpu.make_async_remote_copy(
            src_ref=src, dst_ref=dst, send_sem=send, recv_sem=recv, device_id={axis: to}, device_id_type=MESH
        )

    up_cols, down_cols = up_in.shape[-1], down_in.shape[-2]

    def shard(l, kind, owner):
        if kind == 0:
            return upg[l].at[:, :, :, pl.ds(pl.multiple_of(owner * up_cols, up_cols), up_cols)]
        return downg[l].at[:, :, pl.ds(pl.multiple_of(owner * down_cols, down_cols), down_cols), :]

    def weight_copy(l, kind, way):
        src = (up_in if kind == 0 else down_in).at[l]
        if way == 0:
            return pltpu.make_async_copy(src, shard(l, kind, me_tok), wloc.at[l, kind])
        if way == 1:
            to, at = chip_peer, shard(l, kind, me_tok)
        elif way == 2:
            to, at = core_peer, shard(l, kind, me_tok)
        else:
            src = at = shard(l, kind, chip_peer)
            to = core_peer
        return remote(src, at, wsend.at[l, kind, way - 1], wrecv.at[l, kind, way - 1], "tok", to)

    def start_weights(l):
        for kind in range(2):
            for way in range(3):
                weight_copy(l, kind, way).start()

    shared = set()

    def share_weights(l, kind):
        if (l, kind) in shared:
            return
        shared.add((l, kind))
        weight_copy(l, kind, 1).wait_recv()
        weight_copy(l, kind, 3).start()

    quarter = rank // n_tok

    def out_rows(slot, owner):
        at = pl.ds(pl.multiple_of(owner * quarter, quarter), quarter)
        return outs.at[:, :, at, :] if slot is None else outs.at[slot, :, at, :]

    def share_copy(way):
        at = out_rows(None, chip_peer if way == 2 else me_tok)
        return remote(at, at, qsend.at[way], qrecv.at[way], "tok", core_peer if way else chip_peer)

    def share_outs():
        share_copy(0).wait_recv()
        share_copy(2).start()

    prepared = set()

    def prepare(l, kind):
        if (l, kind) in prepared:
            return
        prepared.add((l, kind))
        share_weights(l, kind)
        weight_copy(l, kind, 0).wait()
        weight_copy(l, kind, 2).wait_recv()
        weight_copy(l, kind, 3).wait_recv()
        order = []
        for b in range(levels):
            at = 0
            for k in range(levels):
                at = jnp.maximum(at, jnp.where(level_bits[l, k] == b, 1 + k, 0))
            order.append(at)
        for j in range(blocks):
            if kind == 0:
                wup[l, j, pl.ds(0, wb), :] = upg[l][j, 0]
                for b in range(levels):
                    wup[l, j, pl.ds((1 + b) * wb, wb), :] = upg[l][j, order[b]]
            else:
                wdown[l, j, pl.ds(0, wb), :] = downg[l][j, 0]
                for b in range(levels):
                    wdown[l, j, pl.ds((1 + b) * wb, wb), :] = downg[l][j, order[b]]

    def rows_of(c):
        return pl.ds(starts[c], sizes[c])

    def own_x(l):
        return xbuf.at[l]

    WAYS = (("own", 0, across), ("own", 1, near), ("own", 3, cross), (1, 2, cross), (3, 2, near), (2, 3, near))

    def x_copy(l, c, way):
        src, slot, to = WAYS[way]
        if c == chunks:
            at = pl.ds(pl.multiple_of(me_tok * quarter, quarter), quarter)
            src = all_out.at[:, at, :] if src == "own" else out_rows(src - 1, me_tok)
            return remote(src, out_rows(slot - 1, me_tok), osend.at[way], orecv.at[slot], "feat", to)
        at = rows_of(c)
        src = (xbuf.at[l] if l else tokens).at[at, :] if src == "own" else xrecv.at[l, src, at, :]
        return remote(src, xrecv.at[l, slot, at, :], xs_sem.at[l, c, way], xr_sem.at[l, c, slot], "feat", to)

    T_WAYS = ((0, 0, across), (1, 1, near), (2, 2, near), (3, 3, near), (2, 4, cross), (3, 5, cross))

    def t_copy(l, c, way):
        src, slot, to = T_WAYS[way]
        at = rows_of(c)
        return remote(
            tsend.at[l, src, at, :], trecv.at[l, slot, at, :], ts_sem.at[l, c, way], tr_sem.at[l, c, slot], "feat", to
        )

    def pair_copy(u, c):
        at = rows_of(c)
        return remote(part.at[u, at, :], got.at[u, at, :], as_sem.at[u, c], ar_sem.at[u, c], "feat", across)

    def pair_sum(u, c):
        pair_copy(u, c).wait_recv()
        at = rows_of(c)
        total = part[u, at, :].astype(jnp.float32) + got[u, at, :].astype(jnp.float32)
        full[u, at, :] = total.astype(jnp.bfloat16)

    def send_cross(l, c):
        @inner
        def _():
            x_copy(l, c, 2).start()

    def send_near(l, c):
        x_copy(l, c, 1).start()

    def send_across(l, c):
        x_copy(l, c, 0).start()

    def relay_in(l, c):
        x_copy(l, c, 1).wait_recv()

        @inner
        def _():
            x_copy(l, c, 3).start()

    def relay_cross(l, c):
        @inner
        def _():
            x_copy(l, c, 2).wait_recv()
            x_copy(l, c, 4).start()

    def relay_out(l, c):
        @inner
        def _():
            x_copy(l, c, 3).wait_recv()
            x_copy(l, c, 5).start()

    def line_done(l, c):
        @outer
        def _():
            x_copy(l, c, 4).wait_recv()
            x_copy(l, c, 5).wait_recv()

    def begin(l, c):
        line_done(l, c)
        if c == chunks:
            share_copy(0).start()
            share_copy(1).start()
            return
        loaded("x", "in")
        at = rows_of(c)
        total = None
        for slot, owner in ((0, me), (1, near), (2, far), (3, cross)):
            x = xrecv[l, slot, at, :] if slot else own_x(l)[at, :]
            term = jnp.dot(
                x, rank_in[l, pl.ds(pl.multiple_of(owner * width, width), width), :],
                preferred_element_type=jnp.float32,
            )
            total = term if total is None else total + term
        part[2 * l, at, :] = total.astype(jnp.bfloat16)
        pair_copy(2 * l, c).start()

    def latent(l, c):
        if c == chunks:
            return share_weights(0, 0)
        pair_sum(2 * l, c)

    def up(l, c):
        if c == chunks:
            return share_weights(0, 1)
        at = rows_of(c)
        xin = own_x(l)
        prepare(l, 0)
        loaded("down", ("up", l))
        x_copy(l, c, 0).wait_recv()
        for j in range(blocks):
            pieces = [xin[at, pl.ds(j * wb, wb)]]
            for b in range(local_bits):
                pieces.append(xin[at, pl.ds((j ^ (1 << b)) * wb, wb)])
            for b in range(nb):
                pieces.append(xrecv[l, b, at, pl.ds(j * wb, wb)])
            pieces.append(full[2 * l, at, :])
            pre = jnp.dot(
                jnp.concatenate(pieces, axis=1), wup[l, j], preferred_element_type=jnp.float32
            )
            act = 0.5 * pre * (1.0 + lax.erf(pre * (1.0 / math.sqrt(2.0))))
            hid[at, pl.ds(j * hb, hb)] = act.astype(jnp.bfloat16)
        part[2 * l + 1, at, :] = jnp.dot(
            hid[at, :], rank_down[l], preferred_element_type=jnp.float32
        ).astype(jnp.bfloat16)
        pair_copy(2 * l + 1, c).start()

    def down(l, c):
        if c == chunks:
            return share_outs()
        at = rows_of(c)
        xin = own_x(l)
        prepare(l, 1)
        own = [None] * blocks
        for j in range(blocks):
            col = pl.ds(j * wb, wb)
            out_j = lax.dot_general(
                hid[at, pl.ds(j * hb, hb)],
                wdown[l, j],
                (((1,), (1,)), ((), ())),
                preferred_element_type=jnp.float32,
            )
            terms = [out_j[:, k * wb : (k + 1) * wb] for k in range(1 + levels)]
            tsend[l, 0, at, col] = terms[1 + local_bits].astype(jnp.bfloat16)
            for b in range(1, nb):
                terms_to[b - 1, at, col] = terms[1 + local_bits + b]
            for to, value in [(j, terms[0])] + [(j ^ (1 << b), terms[1 + b]) for b in range(local_bits)]:
                own[to] = value if own[to] is None else own[to] + value
        for j in range(blocks):
            col = pl.ds(j * wb, wb)
            acc[at, col] = own[j] + xin[at, col].astype(jnp.float32)

    def send_t_across(l, c):
        t_copy(l, c, 0).start()

    outs_ready = set()

    def low_rank(l, c):
        if not outs_ready:
            outs_ready.add(0)
            loaded("out")
            share_copy(1).wait_recv()
            share_copy(2).wait_recv()
        at = rows_of(c)
        pair_sum(2 * l + 1, c)
        low = full[2 * l + 1, at, :]

        def term(slot):
            return jnp.dot(low, outs[slot - 1, l], preferred_element_type=jnp.float32)

        @inner
        def _():
            for slot in (1, 2):
                terms_to[slot - 1, at, :] += term(slot)
            terms_to[2, at, :] = term(3)

        @outer
        def _():
            tsend[l, 3, at, :] = term(3).astype(jnp.bfloat16)
            t_copy(l, c, 3).start()
            for slot in (2, 1):
                tsend[l, slot, at, :] = (terms_to[slot - 1, at, :] + term(slot)).astype(jnp.bfloat16)
                t_copy(l, c, slot).start()

        acc[at, :] += jnp.dot(low, rank_out[l], preferred_element_type=jnp.float32)

    def pass_on(l, c, slot, way):
        at = rows_of(c)

        @inner
        def _():
            t_copy(l, c, {3: 3, 2: 2, 4: 4}[slot]).wait_recv()
            src = T_WAYS[way][0]
            total = terms_to[src - 1, at, :] + trecv[l, slot, at, :].astype(jnp.float32)
            tsend[l, src, at, :] = total.astype(jnp.bfloat16)
            t_copy(l, c, way).start()

    def pass_far(l, c):
        pass_on(l, c, 3, 4)

    def pass_cross(l, c):
        pass_on(l, c, 2, 5)

    def pass_out(l, c):
        pass_on(l, c, 4, 1)

    def close(l, c):
        at = rows_of(c)

        @inner
        def _():
            t_copy(l, c, 5).wait_recv()
            acc[at, :] += trecv[l, 5, at, :].astype(jnp.float32)

        t_copy(l, c, 0).wait_recv()
        t_copy(l, c, 1).wait_recv()
        total = acc[at, :]
        for slot in range(2):
            total = total + trecv[l, slot, at, :].astype(jnp.float32)
        result = total.astype(jnp.bfloat16)
        if l + 1 < layers:
            xbuf[l + 1, at, :] = result
        else:
            out[at, :] = result

    steps = [
        send_cross, send_near, send_across, relay_in, relay_cross, relay_out, begin, latent, up, down,
        send_t_across, low_rank, pass_far, pass_cross, pass_out, close,
    ]
    weights_left = list(range(layers))
    for at, (step, l, c) in enumerate(line_order(layers, chunks)):
        steps[step](l, c)
        if at == 2:
            start_weights(weights_left.pop(0))
        if (step, c) == (9, chunks):
            while weights_left:
                start_weights(weights_left.pop(0))

    for l in range(layers):
        for kind in range(2):
            for way in range(1, 4):
                weight_copy(l, kind, way).wait_send()
        for c in range(chunks + (l == 0)):
            x_copy(l, c, 1).wait_send()

            @inner
            def _():
                for way in range(2, 6):
                    x_copy(l, c, way).wait_send()

            if c == chunks:
                continue
            x_copy(l, c, 0).wait_send()
            for way in range(2):
                t_copy(l, c, way).wait_send()

            @inner
            def _():
                for way in (4, 5):
                    t_copy(l, c, way).wait_send()

            @outer
            def _():
                for way in (2, 3):
                    t_copy(l, c, way).wait_send()

            for u in (2 * l, 2 * l + 1):
                pair_copy(u, c).wait_send()
    for way in range(3):
        share_copy(way).wait_send()


def per_device(tokens, level_bits, up_blocks, down_blocks, rank_in, rank_up, rank_down, rank_out):
    rows, width = tokens.shape
    layers, blocks, parts, wb, up_cols = up_blocks.shape
    hb, down_cols = down_blocks.shape[3:]
    n_tok, n_feat = lax.axis_size("tok"), lax.axis_size("feat")
    rank = rank_in.shape[-1]
    hidden = blocks * hb
    nb = bits_of(n_feat)
    chunk = min(CHUNK_ROWS, rows)
    chunks = rows // chunk
    gather = n_tok > 1 and up_cols % 128 == 0 and down_cols % 16 == 0
    if not gather:
        up_blocks = lax.all_gather(up_blocks, "tok", axis=4, tiled=True)
        down_blocks = lax.all_gather(down_blocks, "tok", axis=4, tiled=True)
    down_blocks = jnp.swapaxes(down_blocks, 3, 4)
    cfg = dict(
        layers=layers, rows=rows, width=width, blocks=blocks, wb=wb, hb=hb, n_feat=n_feat,
        n_tok=n_tok, rank=rank, chunk=chunk, gather=gather, skew=SKEW,
    )
    bf16 = jnp.bfloat16
    uses = 2 * layers
    half_rows = chunk
    scratch = [
        pltpu.VMEM((layers, rows, width), bf16),
        pltpu.VMEM((layers, nb, rows, width), bf16),
        pltpu.VMEM((layers, nb, rows, width), bf16),
        pltpu.VMEM((layers, nb, rows, width), bf16),
        pltpu.VMEM((uses, rows, rank), bf16),
        pltpu.VMEM((uses, chunks * half_rows, rank), bf16),
        pltpu.VMEM((uses, rows, rank), bf16),
        pltpu.VMEM((rows, hidden), bf16),
        pltpu.VMEM((rows, width), jnp.float32),
        pltpu.VMEM((layers, blocks, parts * wb + rank, hb), bf16),
        pltpu.VMEM((layers, blocks, parts * wb, hb), bf16),
    ]
    dma = pltpu.SemaphoreType.DMA
    line = gather and nb == 3 and n_tok == 4 and rank % (16 * n_tok) == 0 and rows % LINE_CHUNK == 0
    if line:
        sizes = SIZES.get(rows) or (LINE_CHUNK,) * (rows // LINE_CHUNK)
        cfg["sizes"] = sizes
        pieces = len(sizes)
        scratch[1:5] = [
            pltpu.VMEM((layers, nb + 1, rows, width), bf16),
            pltpu.VMEM((layers, nb + 1, rows, width), bf16),
            pltpu.VMEM((layers, 2 * nb, rows, width), bf16),
            pltpu.VMEM((nb, rows, width), jnp.float32),
            pltpu.VMEM((uses, rows, rank), bf16),
        ]
        scratch[6] = pltpu.VMEM((uses, rows, rank), bf16)
        scratch += [
            pltpu.VMEM((nb, layers, rank, width), bf16),
            pltpu.VMEM(rank_in.shape, bf16),
            pltpu.VMEM(rank_down.shape, bf16),
            pltpu.VMEM(rank_out.shape, bf16),
            dma((4 + layers * blocks,)),
        ]
        scratch += [pltpu.VMEM((blocks, parts, wb, hb), bf16)] * (2 * layers)
        scratch += [dma((layers, 2, 3)), dma((layers, 2, 3)), dma((layers, 2)), dma((6,)), dma((4,)), dma((3,)), dma((3,))]
        scratch += [dma((layers, pieces, 6)), dma((layers, pieces, 4)), dma((layers, pieces, 6)), dma((layers, pieces, 6))]
        scratch += [dma((uses, pieces))] * 2
    elif gather:
        scratch += [pltpu.VMEM((blocks, parts, wb, hb), bf16)] * (2 * layers)
        scratch += [
            dma((layers, 2, n_tok - 1)),
            dma((layers, 2, n_tok - 1)),
            dma((layers, 2)),
        ]
    if not line:
        scratch += [dma((layers, chunks, nb))] * 4 + [dma((uses, chunks, 2 * nb - 1))] * 2
    vmem = pl.BlockSpec(memory_space=pltpu.VMEM)
    smem = pl.BlockSpec(memory_space=pltpu.SMEM)
    held = pl.BlockSpec(memory_space=pl.ANY) if line else vmem
    return pl.pallas_call(
        functools.partial(line_network if line else network, cfg),
        out_shape=jax.ShapeDtypeStruct((rows, width), bf16),
        in_specs=[held, smem] + [held] * 6,
        out_specs=vmem,
        scratch_shapes=scratch,
        compiler_params=pltpu.CompilerParams(
            collective_id=0, has_side_effects=True, vmem_limit_bytes=63 * 1024 * 1024
        ),
    )(tokens, level_bits, up_blocks, down_blocks, rank_in, rank_up, rank_down, rank_out)


def solution(mesh):
    return jax.shard_map(
        per_device,
        mesh=mesh,
        in_specs=(
            P("tok", "feat"),
            P(),
            P(None, "feat", None, None, "tok"),
            P(None, "feat", None, None, "tok"),
            P(),
            P(None, None, "feat"),
            P(None, "feat", None),
            P(None, None, "feat"),
        ),
        out_specs=P("tok", "feat"),
        check_vma=False,
    )
```

```python
import functools
import math

import jax
import jax.numpy as jnp
from jax import lax
from jax.experimental import pallas as pl
from jax.experimental.pallas import tpu as pltpu
from jax.sharding import PartitionSpec as P

CHUNK_ROWS = 256
LINE_CHUNK = 128
SKEW = 1
LATER = 1
MESH = pl.DeviceIdType.MESH


def bits_of(count):
    return count.bit_length() - 1


def network(cfg, tokens, level_bits, up_in, down_in, rank_in, rank_up, rank_down, rank_out, out, *scratch):
    (xbuf, xrecv, tsend, trecv, part, half, full, hid, acc, wup, wdown) = scratch[:11]
    rest = scratch[11:]
    layers, rows, width = cfg["layers"], cfg["rows"], cfg["width"]
    blocks, wb, hb = cfg["blocks"], cfg["wb"], cfg["hb"]
    n_feat, n_tok, rank = cfg["n_feat"], cfg["n_tok"], cfg["rank"]
    cr = cfg["chunk"]
    chunks = rows // cr
    local_bits = bits_of(blocks)
    nb = bits_of(n_feat)
    levels = local_bits + nb
    gather = cfg["gather"]
    if gather:
        upg, downg = rest[:layers], rest[layers : 2 * layers]
        wsend, wrecv, wloc = rest[2 * layers : 2 * layers + 3]
        rest = rest[2 * layers + 3 :]
    else:
        upg = [up_in.at[l] for l in range(layers)]
        downg = [down_in.at[l] for l in range(layers)]
    xs_sem, xr_sem, ts_sem, tr_sem, as_sem, ar_sem = rest

    me = lax.axis_index("feat")
    me_tok = lax.axis_index("tok")
    mybit = [(me // (1 << b)) % 2 for b in range(nb)]
    partner = [me + (1 << b) * (1 - 2 * mybit[b]) for b in range(nb)]

    barrier = pltpu.get_barrier_semaphore()
    for b in range(nb):
        pl.semaphore_signal(barrier, inc=1, device_id={"feat": partner[b]}, device_id_type=MESH)
    greeted = nb
    if gather:
        for o in range(1, n_tok):
            pl.semaphore_signal(
                barrier, inc=1, device_id={"tok": lax.rem(me_tok + o, n_tok)}, device_id_type=MESH
            )
        greeted += n_tok - 1
    pl.semaphore_wait(barrier, greeted)

    def weight_copy(l, kind, o):
        if kind == 0:
            cols = up_in.shape[-1]
            src = up_in.at[l]
            dst = upg[l].at[:, :, :, pl.ds(pl.multiple_of(me_tok * cols, cols), cols)]
        else:
            cols = down_in.shape[-2]
            src = down_in.at[l]
            dst = downg[l].at[:, :, pl.ds(pl.multiple_of(me_tok * cols, cols), cols), :]
        if o == 0:
            return pltpu.make_async_copy(src, dst, wloc.at[l, kind])
        return pltpu.make_async_remote_copy(
            src_ref=src,
            dst_ref=dst,
            send_sem=wsend.at[l, kind, o - 1],
            recv_sem=wrecv.at[l, kind, o - 1],
            device_id={"tok": lax.rem(me_tok + o, n_tok)},
            device_id_type=MESH,
        )

    def start_weights():
        for l in range(layers):
            for kind in range(2):
                for o in range(n_tok):
                    weight_copy(l, kind, o).start()

    prepared = set()

    def prepare(l, kind):
        if (l, kind) in prepared:
            return
        prepared.add((l, kind))
        if gather:
            for o in range(n_tok):
                copy = weight_copy(l, kind, o)
                copy.wait() if o == 0 else copy.wait_recv()
        order = []
        for b in range(levels):
            at = 0
            for k in range(levels):
                at = jnp.maximum(at, jnp.where(level_bits[l, k] == b, 1 + k, 0))
            order.append(at)
        for j in range(blocks):
            if kind == 0:
                wup[l, j, pl.ds(0, wb), :] = upg[l][j, 0]
                for b in range(levels):
                    wup[l, j, pl.ds((1 + b) * wb, wb), :] = upg[l][j, order[b]]
                wup[l, j, pl.ds((1 + levels) * wb, rank), :] = rank_up[l, :, pl.ds(j * hb, hb)]
            else:
                wdown[l, j, pl.ds(0, wb), :] = downg[l][j, 0]
                for b in range(levels):
                    wdown[l, j, pl.ds((1 + b) * wb, wb), :] = downg[l][j, order[b]]

    def x_copy(l, c, b):
        at = pl.ds(c * cr, cr)
        return pltpu.make_async_remote_copy(
            src_ref=xbuf.at[l, at, :],
            dst_ref=xrecv.at[l, b, at, :],
            send_sem=xs_sem.at[l, c, b],
            recv_sem=xr_sem.at[l, c, b],
            device_id={"feat": partner[b]},
            device_id_type=MESH,
        )

    def t_copy(l, c, b):
        at = pl.ds(c * cr, cr)
        return pltpu.make_async_remote_copy(
            src_ref=tsend.at[l, b, at, :],
            dst_ref=trecv.at[l, b, at, :],
            send_sem=ts_sem.at[l, c, b],
            recv_sem=tr_sem.at[l, c, b],
            device_id={"feat": partner[b]},
            device_id_type=MESH,
        )

    last = nb - 1
    sizes = [cr >> (k + 1) for k in range(last)]
    own_at = [0]
    for k in range(last):
        own_at.append(own_at[-1] + mybit[k] * sizes[k])
    away_at = [own_at[k] + (1 - mybit[k]) * sizes[k] for k in range(last)]
    piece = cr >> last
    half_at = [sum(sizes[:k]) for k in range(last + 1)]
    half_rows = half_at[-1] + piece

    def reduce_copy(u, c, k):
        if k < last:
            src = part.at[u, pl.ds(pl.multiple_of(c * cr + away_at[k], sizes[k]), sizes[k]), :]
            size = sizes[k]
        else:
            src = part.at[u, pl.ds(pl.multiple_of(c * cr + own_at[last], piece), piece), :]
            size = piece
        return pltpu.make_async_remote_copy(
            src_ref=src,
            dst_ref=half.at[u, pl.ds(c * half_rows + half_at[k], size), :],
            send_sem=as_sem.at[u, c, k],
            recv_sem=ar_sem.at[u, c, k],
            device_id={"feat": partner[k]},
            device_id_type=MESH,
        )

    def spread_copy(u, c, k):
        size = cr >> (k + 1)
        at = pl.ds(pl.multiple_of(c * cr + own_at[k + 1], size), size)
        return pltpu.make_async_remote_copy(
            src_ref=full.at[u, at, :],
            dst_ref=full.at[u, at, :],
            send_sem=as_sem.at[u, c, nb + k],
            recv_sem=ar_sem.at[u, c, nb + k],
            device_id={"feat": partner[k]},
            device_id_type=MESH,
        )

    def start_bulk(u, c, stage):
        for b in reversed(range(nb)):
            if min(LATER, nb) * (0 if b == last else 1) == stage:
                (t_copy if u % 2 else x_copy)(u // 2, c, b).start()

    def sum_stage(u, c, k):
        reduce_copy(u, c, k).wait_recv()
        size = sizes[k] if k < last else piece
        start = own_at[k + 1] if k < last else own_at[last]
        at = pl.ds(pl.multiple_of(c * cr + start, size), size)
        total = part[u, at, :].astype(jnp.float32) + half[
            u, pl.ds(c * half_rows + half_at[k], size), :
        ].astype(jnp.float32)
        if k < last:
            part[u, at, :] = total.astype(jnp.bfloat16)
            reduce_copy(u, c, k + 1).start()
        else:
            full[u, at, :] = total.astype(jnp.bfloat16)
            if last > 0:
                spread_copy(u, c, last - 1).start()
        start_bulk(u, c, k + 1)

    def spread_stage(u, c, k):
        spread_copy(u, c, k).wait_recv()
        if k > 0:
            spread_copy(u, c, k - 1).start()

    def sum_stages(u, c):
        found = [functools.partial(sum_stage, u, c, k) for k in range(nb)]
        for k in range(last - 1, 0, -1):
            found.append(functools.partial(spread_stage, u, c, k))
        return found

    def finish_sum(u, c):
        if last > 0:
            spread_stage(u, c, 0)

    def begin(l, c):
        at = pl.ds(c * cr, cr)
        u = 2 * l
        x = xbuf[l, at, :]
        mine = rank_in[l, pl.ds(pl.multiple_of(me * width, width), width), :]
        part[u, at, :] = jnp.dot(x, mine, preferred_element_type=jnp.float32).astype(jnp.bfloat16)
        reduce_copy(u, c, 0).start()
        start_bulk(u, c, 0)

    def first(c):
        at = pl.ds(c * cr, cr)
        xbuf[0, at, :] = tokens[at, :]
        begin(0, c)

    def middle(l, c):
        at = pl.ds(c * cr, cr)
        u = 2 * l + 1
        prepare(l, 0)
        finish_sum(u - 1, c)
        for b in range(nb):
            x_copy(l, c, b).wait_recv()
        for j in range(blocks):
            pieces = [xbuf[l, at, pl.ds(j * wb, wb)]]
            for b in range(local_bits):
                pieces.append(xbuf[l, at, pl.ds((j ^ (1 << b)) * wb, wb)])
            for b in range(nb):
                pieces.append(xrecv[l, b, at, pl.ds(j * wb, wb)])
            pieces.append(full[u - 1, at, :])
            pre = jnp.dot(
                jnp.concatenate(pieces, axis=1), wup[l, j], preferred_element_type=jnp.float32
            )
            act = 0.5 * pre * (1.0 + lax.erf(pre * (1.0 / math.sqrt(2.0))))
            hid[at, pl.ds(j * hb, hb)] = act.astype(jnp.bfloat16)
        part[u, at, :] = jnp.dot(
            hid[at, :], rank_down[l], preferred_element_type=jnp.float32
        ).astype(jnp.bfloat16)
        reduce_copy(u, c, 0).start()
        prepare(l, 1)
        own = [None] * blocks
        for j in range(blocks):
            out_j = lax.dot_general(
                hid[at, pl.ds(j * hb, hb)],
                wdown[l, j],
                (((1,), (1,)), ((), ())),
                preferred_element_type=jnp.float32,
            )
            terms = [out_j[:, k * wb : (k + 1) * wb] for k in range(1 + levels)]
            for b in range(nb):
                tsend[l, b, at, pl.ds(j * wb, wb)] = terms[1 + local_bits + b].astype(jnp.bfloat16)
            for to, value in [(j, terms[0])] + [(j ^ (1 << b), terms[1 + b]) for b in range(local_bits)]:
                own[to] = value if own[to] is None else own[to] + value
        start_bulk(u, c, 0)
        for j in range(blocks):
            col = pl.ds(j * wb, wb)
            acc[at, col] = own[j] + xbuf[l, at, col].astype(jnp.float32)

    def close(l, c):
        at = pl.ds(c * cr, cr)
        u = 2 * l + 1
        finish_sum(u, c)
        total = acc[at, :] + jnp.dot(full[u, at, :], rank_out[l], preferred_element_type=jnp.float32)
        for b in range(nb):
            t_copy(l, c, b).wait_recv()
            total = total + trecv[l, b, at, :].astype(jnp.float32)
        result = total.astype(jnp.bfloat16)
        if l + 1 < layers:
            xbuf[l + 1, at, :] = result
            begin(l + 1, c)
        else:
            out[at, :] = result

    plan = []
    for c in range(chunks):
        steps = [functools.partial(first, c)]
        for l in range(layers):
            steps += sum_stages(2 * l, c)
            steps.append(functools.partial(middle, l, c))
            steps += sum_stages(2 * l + 1, c)
            steps.append(functools.partial(close, l, c))
        plan.append(steps)

    plan[0][0]()
    if gather:
        start_weights()
    for tick in range(1, len(plan[0]) + cfg["skew"] * (chunks - 1)):
        for c in range(chunks):
            at = tick - cfg["skew"] * c
            if 0 <= at < len(plan[c]):
                plan[c][at]()

    for l in range(layers):
        if gather:
            for kind in range(2):
                for o in range(1, n_tok):
                    weight_copy(l, kind, o).wait_send()
        for c in range(chunks):
            for b in range(nb):
                x_copy(l, c, b).wait_send()
                t_copy(l, c, b).wait_send()
            for u in (2 * l, 2 * l + 1):
                for k in range(nb):
                    reduce_copy(u, c, k).wait_send()
                for k in range(last):
                    spread_copy(u, c, k).wait_send()


ORDERS = {
    (2, 7): (
        16, 32, 1, 17, 0, 7, 23, 36, 34, 37, 18, 48, 22, 19, 4, 49,
        55, 71, 54, 80, 64, 2, 50, 33, 65, 81, 51, 119, 87, 96, 103, 97,
        21, 5, 20, 3, 66, 112, 35, 6, 135, 128, 113, 129, 68, 151, 144, 160,
        176, 52, 82, 98, 38, 145, 177, 161, 83, 114, 53, 130, 146, 67, 99, 192,
        162, 70, 208, 84, 178, 100, 224, 86, 193, 240, 115, 131, 209, 288, 272, 256,
        102, 194, 225, 116, 147, 241, 179, 85, 132, 210, 69, 101, 289, 273, 226, 148,
        320, 118, 134, 195, 242, 274, 257, 304, 180, 117, 133, 163, 164, 290, 211, 227,
        305, 149, 181, 258, 150, 243, 275, 337, 196, 291, 336, 352, 212, 321, 353, 322,
        166, 182, 306, 165, 228, 244, 292, 213, 260, 276, 369, 197, 385, 338, 368, 384,
        354, 401, 417, 433, 198, 229, 400, 308, 245, 277, 261, 230, 324, 214, 370, 386,
        416, 340, 259, 402, 418, 246, 294, 307, 449, 356, 278, 432, 323, 293, 434, 325,
        262, 339, 355, 309, 372, 388, 404, 310, 341, 357, 371, 387, 403, 436, 448, 326,
        450, 342, 480, 358, 435, 373, 419, 464, 389, 465, 452, 374, 390, 482, 466, 451,
        481, 406, 467, 420, 468, 484, 438, 496, 405, 421, 437, 422, 454, 483, 498, 453,
        470, 469, 500, 497, 486, 485, 502, 499, 501,
    ),
}
SIZES = {
    1024: (128, 128, 160, 160, 160, 160, 128),
}


def line_order(layers, chunks):
    found = ORDERS.get((layers, chunks))
    if found is not None:
        return [(code // 16 % 16, code // 256, code % 16) for code in found]
    groups = [[3, 4], [5], [6], [7, 8, 9, 10], [11], [12, 13], [14], [15]]
    ticks = [[(step, 0) for step in range(3)]]
    for l in range(layers):
        ticks += [[(step, l) for step in group] for group in groups]
        if l + 1 < layers:
            ticks[-1] += [(step, l + 1) for step in range(3)]
    order = []
    for tick in range(len(ticks) + chunks - 1):
        for c in range(chunks):
            if 0 <= tick - c < len(ticks):
                order += [(step, l, c) for step, l in ticks[tick - c]]
    at = order.index((2, 0, 0)) + 1
    order[at:at] = [(0, 0, chunks), (1, 0, chunks)]
    at = order.index((6, 0, 0)) + 1
    order[at:at] = [(3, 0, chunks), (4, 0, chunks)]
    at = order.index((6, 0, min(1, chunks - 1))) + 1
    order[at:at] = [(5, 0, chunks), (6, 0, chunks), (7, 0, chunks), (8, 0, chunks)]
    at = order.index((11, 0, 0))
    order[at:at] = [(9, 0, chunks)]
    return order


def line_network(cfg, tokens, level_bits, up_in, down_in, all_in, all_up, all_down, all_out, out, *scratch):
    (xbuf, xrecv, tsend, trecv, terms_to, part, got, full, hid, acc, wup, wdown, outs) = scratch[:13]
    rank_in, rank_down, rank_out, load_sem = scratch[13:17]
    rest = scratch[17:]
    layers, rows, width = cfg["layers"], cfg["rows"], cfg["width"]
    blocks, wb, hb = cfg["blocks"], cfg["wb"], cfg["hb"]
    n_tok, rank, sizes = cfg["n_tok"], cfg["rank"], cfg["sizes"]
    chunks = len(sizes)
    starts = [sum(sizes[:c]) for c in range(chunks)]
    local_bits = bits_of(blocks)
    nb = 3
    levels = local_bits + nb
    upg, downg = rest[:layers], rest[layers : 2 * layers]
    wsend, wrecv, wloc, osend, orecv, qsend, qrecv = rest[2 * layers : 2 * layers + 7]
    xs_sem, xr_sem, ts_sem, tr_sem, as_sem, ar_sem = rest[2 * layers + 7 :]

    me = lax.axis_index("feat")
    me_tok = lax.axis_index("tok")
    bit = [(me // (1 << b)) % 2 for b in range(nb)]
    flip = [(1 << b) * (1 - 2 * bit[b]) for b in range(nb)]
    across, near, far = [me + flip[b] for b in range(nb)]
    cross = me + flip[1] + flip[2]
    is_inner = bit[1] + bit[2] == 1
    is_outer = bit[1] + bit[2] != 1
    core_peer = me_tok + 1 - 2 * (me_tok % 2)
    chip_peer = me_tok + 2 - 4 * ((me_tok // 2) % 2)

    def inner(f):
        pl.when(is_inner)(f)

    def outer(f):
        pl.when(is_outer)(f)

    low = (1 + levels) * wb
    loads = {"x": [(tokens, xbuf.at[0])], "in": [(all_in, rank_in)]}
    for l in range(layers):
        loads["up", l] = [
            (all_up.at[l, :, pl.ds(j * hb, hb)], wup.at[l, j, pl.ds(low, rank), :]) for j in range(blocks)
        ]
    loads["down"] = [(all_down, rank_down)]
    loads["out"] = [(all_out, rank_out)]
    pending, count = {}, 0
    for name, pairs in loads.items():
        pending[name] = []
        for src, dst in pairs:
            pending[name].append(pltpu.make_async_copy(src, dst, load_sem.at[count]))
            count += 1

    def loaded(*names):
        for name in names:
            for copy in pending.pop(name, ()):
                copy.wait()

    barrier = pltpu.get_barrier_semaphore()
    for to in (across, near):
        pl.semaphore_signal(barrier, inc=1, device_id={"feat": to}, device_id_type=MESH)
    for to in (core_peer, chip_peer):
        pl.semaphore_signal(barrier, inc=1, device_id={"tok": to}, device_id_type=MESH)

    for name in pending:
        for copy in pending[name]:
            copy.start()

    @inner
    def _():
        pl.semaphore_signal(barrier, inc=1, device_id={"feat": cross}, device_id_type=MESH)
        pl.semaphore_wait(barrier, 5)

    @outer
    def _():
        pl.semaphore_wait(barrier, 4)

    def remote(src, dst, send, recv, axis, to):
        return pltpu.make_async_remote_copy(
            src_ref=src, dst_ref=dst, send_sem=send, recv_sem=recv, device_id={axis: to}, device_id_type=MESH
        )

    up_cols, down_cols = up_in.shape[-1], down_in.shape[-2]

    def shard(l, kind, owner):
        if kind == 0:
            return upg[l].at[:, :, :, pl.ds(pl.multiple_of(owner * up_cols, up_cols), up_cols)]
        return downg[l].at[:, :, pl.ds(pl.multiple_of(owner * down_cols, down_cols), down_cols), :]

    def weight_copy(l, kind, way):
        src = (up_in if kind == 0 else down_in).at[l]
        if way == 0:
            return pltpu.make_async_copy(src, shard(l, kind, me_tok), wloc.at[l, kind])
        if way == 1:
            to, at = chip_peer, shard(l, kind, me_tok)
        elif way == 2:
            to, at = core_peer, shard(l, kind, me_tok)
        else:
            src = at = shard(l, kind, chip_peer)
            to = core_peer
        return remote(src, at, wsend.at[l, kind, way - 1], wrecv.at[l, kind, way - 1], "tok", to)

    def start_weights(l):
        for kind in range(2):
            for way in range(3):
                weight_copy(l, kind, way).start()

    shared = set()

    def share_weights(l, kind):
        if (l, kind) in shared:
            return
        shared.add((l, kind))
        weight_copy(l, kind, 1).wait_recv()
        weight_copy(l, kind, 3).start()

    quarter = rank // n_tok

    def out_rows(slot, owner):
        at = pl.ds(pl.multiple_of(owner * quarter, quarter), quarter)
        return outs.at[:, :, at, :] if slot is None else outs.at[slot, :, at, :]

    def share_copy(way):
        at = out_rows(None, chip_peer if way == 2 else me_tok)
        return remote(at, at, qsend.at[way], qrecv.at[way], "tok", core_peer if way else chip_peer)

    def share_outs():
        share_copy(0).wait_recv()
        share_copy(2).start()

    prepared = set()

    def prepare(l, kind):
        if (l, kind) in prepared:
            return
        prepared.add((l, kind))
        share_weights(l, kind)
        weight_copy(l, kind, 0).wait()
        weight_copy(l, kind, 2).wait_recv()
        weight_copy(l, kind, 3).wait_recv()
        order = []
        for b in range(levels):
            at = 0
            for k in range(levels):
                at = jnp.maximum(at, jnp.where(level_bits[l, k] == b, 1 + k, 0))
            order.append(at)
        for j in range(blocks):
            if kind == 0:
                wup[l, j, pl.ds(0, wb), :] = upg[l][j, 0]
                for b in range(levels):
                    wup[l, j, pl.ds((1 + b) * wb, wb), :] = upg[l][j, order[b]]
            else:
                wdown[l, j, pl.ds(0, wb), :] = downg[l][j, 0]
                for b in range(levels):
                    wdown[l, j, pl.ds((1 + b) * wb, wb), :] = downg[l][j, order[b]]

    def rows_of(c):
        return pl.ds(starts[c], sizes[c])

    def own_x(l):
        return xbuf.at[l]

    WAYS = (("own", 0, across), ("own", 1, near), ("own", 3, cross), (1, 2, cross), (3, 2, near), (2, 3, near))

    def x_copy(l, c, way):
        src, slot, to = WAYS[way]
        if c == chunks:
            at = pl.ds(pl.multiple_of(me_tok * quarter, quarter), quarter)
            src = all_out.at[:, at, :] if src == "own" else out_rows(src - 1, me_tok)
            return remote(src, out_rows(slot - 1, me_tok), osend.at[way], orecv.at[slot], "feat", to)
        at = rows_of(c)
        src = (xbuf.at[l] if l else tokens).at[at, :] if src == "own" else xrecv.at[l, src, at, :]
        return remote(src, xrecv.at[l, slot, at, :], xs_sem.at[l, c, way], xr_sem.at[l, c, slot], "feat", to)

    T_WAYS = ((0, 0, across), (1, 1, near), (2, 2, near), (3, 3, near), (2, 4, cross), (3, 5, cross))

    def t_copy(l, c, way):
        src, slot, to = T_WAYS[way]
        at = rows_of(c)
        return remote(
            tsend.at[l, src, at, :], trecv.at[l, slot, at, :], ts_sem.at[l, c, way], tr_sem.at[l, c, slot], "feat", to
        )

    def pair_copy(u, c):
        at = rows_of(c)
        return remote(part.at[u, at, :], got.at[u, at, :], as_sem.at[u, c], ar_sem.at[u, c], "feat", across)

    def pair_sum(u, c):
        pair_copy(u, c).wait_recv()
        at = rows_of(c)
        total = part[u, at, :].astype(jnp.float32) + got[u, at, :].astype(jnp.float32)
        full[u, at, :] = total.astype(jnp.bfloat16)

    def send_cross(l, c):
        @inner
        def _():
            x_copy(l, c, 2).start()

    def send_near(l, c):
        x_copy(l, c, 1).start()

    def send_across(l, c):
        x_copy(l, c, 0).start()

    def relay_in(l, c):
        x_copy(l, c, 1).wait_recv()

        @inner
        def _():
            x_copy(l, c, 3).start()

    def relay_cross(l, c):
        @inner
        def _():
            x_copy(l, c, 2).wait_recv()
            x_copy(l, c, 4).start()

    def relay_out(l, c):
        @inner
        def _():
            x_copy(l, c, 3).wait_recv()
            x_copy(l, c, 5).start()

    def line_done(l, c):
        @outer
        def _():
            x_copy(l, c, 4).wait_recv()
            x_copy(l, c, 5).wait_recv()

    def begin(l, c):
        line_done(l, c)
        if c == chunks:
            share_copy(0).start()
            share_copy(1).start()
            return
        loaded("x", "in")
        at = rows_of(c)
        total = None
        for slot, owner in ((0, me), (1, near), (2, far), (3, cross)):
            x = xrecv[l, slot, at, :] if slot else own_x(l)[at, :]
            term = jnp.dot(
                x, rank_in[l, pl.ds(pl.multiple_of(owner * width, width), width), :],
                preferred_element_type=jnp.float32,
            )
            total = term if total is None else total + term
        part[2 * l, at, :] = total.astype(jnp.bfloat16)
        pair_copy(2 * l, c).start()

    def latent(l, c):
        if c == chunks:
            return share_weights(0, 0)
        pair_sum(2 * l, c)

    def up(l, c):
        if c == chunks:
            return share_weights(0, 1)
        at = rows_of(c)
        xin = own_x(l)
        prepare(l, 0)
        loaded("down", ("up", l))
        x_copy(l, c, 0).wait_recv()
        for j in range(blocks):
            pieces = [xin[at, pl.ds(j * wb, wb)]]
            for b in range(local_bits):
                pieces.append(xin[at, pl.ds((j ^ (1 << b)) * wb, wb)])
            for b in range(nb):
                pieces.append(xrecv[l, b, at, pl.ds(j * wb, wb)])
            pieces.append(full[2 * l, at, :])
            pre = jnp.dot(
                jnp.concatenate(pieces, axis=1), wup[l, j], preferred_element_type=jnp.float32
            )
            act = 0.5 * pre * (1.0 + lax.erf(pre * (1.0 / math.sqrt(2.0))))
            hid[at, pl.ds(j * hb, hb)] = act.astype(jnp.bfloat16)
        part[2 * l + 1, at, :] = jnp.dot(
            hid[at, :], rank_down[l], preferred_element_type=jnp.float32
        ).astype(jnp.bfloat16)
        pair_copy(2 * l + 1, c).start()

    def down(l, c):
        if c == chunks:
            return share_outs()
        at = rows_of(c)
        xin = own_x(l)
        prepare(l, 1)
        own = [None] * blocks
        for j in range(blocks):
            col = pl.ds(j * wb, wb)
            out_j = lax.dot_general(
                hid[at, pl.ds(j * hb, hb)],
                wdown[l, j],
                (((1,), (1,)), ((), ())),
                preferred_element_type=jnp.float32,
            )
            terms = [out_j[:, k * wb : (k + 1) * wb] for k in range(1 + levels)]
            tsend[l, 0, at, col] = terms[1 + local_bits].astype(jnp.bfloat16)
            for b in range(1, nb):
                terms_to[b - 1, at, col] = terms[1 + local_bits + b]
            for to, value in [(j, terms[0])] + [(j ^ (1 << b), terms[1 + b]) for b in range(local_bits)]:
                own[to] = value if own[to] is None else own[to] + value
        for j in range(blocks):
            col = pl.ds(j * wb, wb)
            acc[at, col] = own[j] + xin[at, col].astype(jnp.float32)

    def send_t_across(l, c):
        t_copy(l, c, 0).start()

    outs_ready = set()

    def low_rank(l, c):
        if not outs_ready:
            outs_ready.add(0)
            loaded("out")
            share_copy(1).wait_recv()
            share_copy(2).wait_recv()
        at = rows_of(c)
        pair_sum(2 * l + 1, c)
        low = full[2 * l + 1, at, :]

        def term(slot):
            return jnp.dot(low, outs[slot - 1, l], preferred_element_type=jnp.float32)

        @inner
        def _():
            for slot in (1, 2):
                terms_to[slot - 1, at, :] += term(slot)
            terms_to[2, at, :] = term(3)

        @outer
        def _():
            tsend[l, 3, at, :] = term(3).astype(jnp.bfloat16)
            t_copy(l, c, 3).start()
            for slot in (2, 1):
                tsend[l, slot, at, :] = (terms_to[slot - 1, at, :] + term(slot)).astype(jnp.bfloat16)
                t_copy(l, c, slot).start()

        acc[at, :] += jnp.dot(low, rank_out[l], preferred_element_type=jnp.float32)

    def pass_on(l, c, slot, way):
        at = rows_of(c)

        @inner
        def _():
            t_copy(l, c, {3: 3, 2: 2, 4: 4}[slot]).wait_recv()
            src = T_WAYS[way][0]
            total = terms_to[src - 1, at, :] + trecv[l, slot, at, :].astype(jnp.float32)
            tsend[l, src, at, :] = total.astype(jnp.bfloat16)
            t_copy(l, c, way).start()

    def pass_far(l, c):
        pass_on(l, c, 3, 4)

    def pass_cross(l, c):
        pass_on(l, c, 2, 5)

    def pass_out(l, c):
        pass_on(l, c, 4, 1)

    def close(l, c):
        at = rows_of(c)

        @inner
        def _():
            t_copy(l, c, 5).wait_recv()
            acc[at, :] += trecv[l, 5, at, :].astype(jnp.float32)

        t_copy(l, c, 0).wait_recv()
        t_copy(l, c, 1).wait_recv()
        total = acc[at, :]
        for slot in range(2):
            total = total + trecv[l, slot, at, :].astype(jnp.float32)
        result = total.astype(jnp.bfloat16)
        if l + 1 < layers:
            xbuf[l + 1, at, :] = result
        else:
            out[at, :] = result

    steps = [
        send_cross, send_near, send_across, relay_in, relay_cross, relay_out, begin, latent, up, down,
        send_t_across, low_rank, pass_far, pass_cross, pass_out, close,
    ]
    weights_left = list(range(layers))
    for at, (step, l, c) in enumerate(line_order(layers, chunks)):
        steps[step](l, c)
        if at == 2:
            start_weights(weights_left.pop(0))
        if (step, c) == (9, chunks):
            while weights_left:
                start_weights(weights_left.pop(0))

    for l in range(layers):
        for kind in range(2):
            for way in range(1, 4):
                weight_copy(l, kind, way).wait_send()
        for c in range(chunks + (l == 0)):
            x_copy(l, c, 1).wait_send()

            @inner
            def _():
                for way in range(2, 6):
                    x_copy(l, c, way).wait_send()

            if c == chunks:
                continue
            x_copy(l, c, 0).wait_send()
            for way in range(2):
                t_copy(l, c, way).wait_send()

            @inner
            def _():
                for way in (4, 5):
                    t_copy(l, c, way).wait_send()

            @outer
            def _():
                for way in (2, 3):
                    t_copy(l, c, way).wait_send()

            for u in (2 * l, 2 * l + 1):
                pair_copy(u, c).wait_send()
    for way in range(3):
        share_copy(way).wait_send()


def per_device(tokens, level_bits, up_blocks, down_blocks, rank_in, rank_up, rank_down, rank_out):
    rows, width = tokens.shape
    layers, blocks, parts, wb, up_cols = up_blocks.shape
    hb, down_cols = down_blocks.shape[3:]
    n_tok, n_feat = lax.axis_size("tok"), lax.axis_size("feat")
    rank = rank_in.shape[-1]
    hidden = blocks * hb
    nb = bits_of(n_feat)
    chunk = min(CHUNK_ROWS, rows)
    chunks = rows // chunk
    gather = n_tok > 1 and up_cols % 128 == 0 and down_cols % 16 == 0
    if not gather:
        up_blocks = lax.all_gather(up_blocks, "tok", axis=4, tiled=True)
        down_blocks = lax.all_gather(down_blocks, "tok", axis=4, tiled=True)
    down_blocks = jnp.swapaxes(down_blocks, 3, 4)
    cfg = dict(
        layers=layers, rows=rows, width=width, blocks=blocks, wb=wb, hb=hb, n_feat=n_feat,
        n_tok=n_tok, rank=rank, chunk=chunk, gather=gather, skew=SKEW,
    )
    bf16 = jnp.bfloat16
    uses = 2 * layers
    half_rows = chunk
    scratch = [
        pltpu.VMEM((layers, rows, width), bf16),
        pltpu.VMEM((layers, nb, rows, width), bf16),
        pltpu.VMEM((layers, nb, rows, width), bf16),
        pltpu.VMEM((layers, nb, rows, width), bf16),
        pltpu.VMEM((uses, rows, rank), bf16),
        pltpu.VMEM((uses, chunks * half_rows, rank), bf16),
        pltpu.VMEM((uses, rows, rank), bf16),
        pltpu.VMEM((rows, hidden), bf16),
        pltpu.VMEM((rows, width), jnp.float32),
        pltpu.VMEM((layers, blocks, parts * wb + rank, hb), bf16),
        pltpu.VMEM((layers, blocks, parts * wb, hb), bf16),
    ]
    dma = pltpu.SemaphoreType.DMA
    line = gather and nb == 3 and n_tok == 4 and rank % (16 * n_tok) == 0 and rows % LINE_CHUNK == 0
    if line:
        sizes = SIZES.get(rows) or (LINE_CHUNK,) * (rows // LINE_CHUNK)
        cfg["sizes"] = sizes
        pieces = len(sizes)
        scratch[1:5] = [
            pltpu.VMEM((layers, nb + 1, rows, width), bf16),
            pltpu.VMEM((layers, nb + 1, rows, width), bf16),
            pltpu.VMEM((layers, 2 * nb, rows, width), bf16),
            pltpu.VMEM((nb, rows, width), jnp.float32),
            pltpu.VMEM((uses, rows, rank), bf16),
        ]
        scratch[6] = pltpu.VMEM((uses, rows, rank), bf16)
        scratch += [
            pltpu.VMEM((nb, layers, rank, width), bf16),
            pltpu.VMEM(rank_in.shape, bf16),
            pltpu.VMEM(rank_down.shape, bf16),
            pltpu.VMEM(rank_out.shape, bf16),
            dma((4 + layers * blocks,)),
        ]
        scratch += [pltpu.VMEM((blocks, parts, wb, hb), bf16)] * (2 * layers)
        scratch += [dma((layers, 2, 3)), dma((layers, 2, 3)), dma((layers, 2)), dma((6,)), dma((4,)), dma((3,)), dma((3,))]
        scratch += [dma((layers, pieces, 6)), dma((layers, pieces, 4)), dma((layers, pieces, 6)), dma((layers, pieces, 6))]
        scratch += [dma((uses, pieces))] * 2
    elif gather:
        scratch += [pltpu.VMEM((blocks, parts, wb, hb), bf16)] * (2 * layers)
        scratch += [
            dma((layers, 2, n_tok - 1)),
            dma((layers, 2, n_tok - 1)),
            dma((layers, 2)),
        ]
    if not line:
        scratch += [dma((layers, chunks, nb))] * 4 + [dma((uses, chunks, 2 * nb - 1))] * 2
    vmem = pl.BlockSpec(memory_space=pltpu.VMEM)
    smem = pl.BlockSpec(memory_space=pltpu.SMEM)
    held = pl.BlockSpec(memory_space=pl.ANY) if line else vmem
    return pl.pallas_call(
        functools.partial(line_network if line else network, cfg),
        out_shape=jax.ShapeDtypeStruct((rows, width), bf16),
        in_specs=[held, smem] + [held] * 6,
        out_specs=vmem,
        scratch_shapes=scratch,
        compiler_params=pltpu.CompilerParams(
            collective_id=0, has_side_effects=True, vmem_limit_bytes=63 * 1024 * 1024
        ),
    )(tokens, level_bits, up_blocks, down_blocks, rank_in, rank_up, rank_down, rank_out)


def solution(mesh):
    return jax.shard_map(
        per_device,
        mesh=mesh,
        in_specs=(
            P("tok", "feat"),
            P(),
            P(None, "feat", None, None, "tok"),
            P(None, "feat", None, None, "tok"),
            P(),
            P(None, None, "feat"),
            P(None, "feat", None),
            P(None, None, "feat"),
        ),
        out_specs=P("tok", "feat"),
        check_vma=False,
    )
```
